32 devices in a mesh: space: 8 (over y, x, core), sample: 4 (over z).
Axes of the slice: x: 2, y: 2, z: 4, core: 2. Of those that a mesh axis runs over, the one named last changes fastest.
Arguments:
- fields: bfloat16 [4, 64, 20, 8192], P('sample', 'space'), may hold values from -6 to 6
- cotangent: bfloat16 [4, 64, 20, 8192], P('sample', 'space'), may hold values from -6 to 6
- spectral_weight: bfloat16 [2, 20, 20, 4608], P(None, None, None, 'space'), may hold values from -6 to 6
- point_weight: bfloat16 [20, 20], replicated, may hold values from -1.25 to 1.25
- point_bias: float32 [20], replicated, may hold values from -1 to 1
Outputs:
- activated: bfloat16 [4, 64, 20, 8192], P('sample', 'space')
- grad_input: bfloat16 [4, 64, 20, 8192], P('sample', 'space')
- grad_spectral: float32 [2, 20, 20, 4608], P(None, None, None, ('space', 'sample'))
The draws below stay inside these ranges and needn't reach their ends.
All inputs are finite; a program needn't handle non-finite values.
Results may differ from the reference program's by a relative error of at most 0.001.
Values sent between devices are 32-bit elements; how exact they have to be, the bound alone decides.
A program may use at most 128 MiB of HBM per device.

```python
import math
import jax
import jax.numpy as jnp
from jax import lax

NX = 64
NY = 64
NZ = 32
NT = 4
C = 20
MX = 12
MY = 12
MZ = 8
MT = 4
SAMPLES = 4
CELLS = 8192
MODES = 4608


def level_of(stream_key, extent, cuts, smallest, top_value):
    gain, own = 1.0, jax.random.fold_in(stream_key, 6)
    for axis_at, blocks in cuts:
        steps = jnp.exp(jax.random.uniform(jax.random.fold_in(own, axis_at), (blocks,), jnp.float32, smallest / len(cuts), top_value / len(cuts)))
        gain = gain * jnp.repeat(steps, extent[axis_at] // blocks).reshape([-1 if axis == axis_at else 1 for axis in range(len(extent))])
    return gain


def scatter_about(own_key, extent, width, limit, pieces=(), kind=jnp.bfloat16):
    factor_of = level_of(own_key, extent, pieces, -0.22, 0.18) if pieces else 1.0
    result = jax.random.normal(own_key, extent, jnp.float32) * width * factor_of
    return jnp.minimum(jnp.maximum(result, -limit), limit).astype(kind)


def setup_inputs(seed: int = 0) -> dict:
    arg_keys = jax.random.split(jax.random.key(seed), 6)
    return {
        "fields": scatter_about(arg_keys[0], (SAMPLES, NX, C, CELLS), 1.0, 6.0, ((0, 4), (1, 8))),
        "cotangent": scatter_about(arg_keys[1], (SAMPLES, NX, C, CELLS), 1.0, 6.0, ((0, 4), (1, 8))),
        "spectral_weight": scatter_about(arg_keys[2], (2, C, C, MODES), 1.0, 6.0, ((3, 8),)),
        "point_weight": scatter_about(arg_keys[3], (C, C), C ** -0.5, 1.25),
        "point_bias": jnp.clip(jax.random.uniform(arg_keys[4], (C,), jnp.float32, -1.0, 1.0), -1.0, 1.0),
    }


def kept_index(length, modes):
    index = jnp.arange(modes, dtype=jnp.int32)
    return jnp.where(index < modes // 2, index, length - modes + index)

def mode_indices():
    index_x = kept_index(NX, MX)[:, None, None, None]
    index_y = kept_index(NY, MY)[None, :, None, None]
    index_z = kept_index(NZ, MZ)[None, None, :, None]
    index_t = kept_index(NT, MT)[None, None, None, :]
    return (index_x, index_y, index_z, index_t)

def to_grid(planes):
    return jnp.transpose(planes, (1, 0, 2)).reshape(planes.shape[1], NX, NY, NZ, NT)

def from_grid(lattice):
    return jnp.transpose(lattice.reshape(lattice.shape[0], NX, NY * NZ * NT), (1, 0, 2))

def select_modes(spectrum):
    index_x, index_y, index_z, index_t = mode_indices()
    picked = spectrum[:, index_x, index_y, index_z, index_t]
    return jnp.transpose(picked, (0, 3, 4, 2, 1)).reshape(spectrum.shape[0], MZ * MT * MY * MX)

def place_modes(coeffs):
    index_x, index_y, index_z, index_t = mode_indices()
    arranged = jnp.transpose(coeffs.reshape(coeffs.shape[0], MZ, MT, MY, MX), (0, 4, 3, 1, 2))
    empty = jnp.zeros((coeffs.shape[0], NX, NY, NZ, NT), dtype=coeffs.dtype)
    return empty.at[:, index_x, index_y, index_z, index_t].set(arranged)

def gelu_slope(values):
    return 0.5 * (1.0 + lax.erf(values * (1.0 / math.sqrt(2.0)))) + values * jnp.exp(-0.5 * values * values) * (1.0 / math.sqrt(2.0 * math.pi))

def reference(fields, cotangent, spectral_weight, point_weight, point_bias):
    volume = NX * NY * NZ * NT
    weights = spectral_weight.astype(jnp.float32)
    mixer_full = weights[0] + 1j * weights[1]
    mixer_conj = weights[0] - 1j * weights[1]
    point_mat = point_weight.astype(jnp.float32)
    bias_vec = point_bias.astype(jnp.float32)
    highest = lax.Precision.HIGHEST

    def per_sample(running, inputs_pair):
        sample_field, sample_cot = inputs_pair
        values = sample_field.astype(jnp.float32)
        spec_in = select_modes(jnp.fft.fftn(to_grid(values), axes=(1, 2, 3, 4)))
        mixed = jnp.einsum('com,cm->om', mixer_full, spec_in, precision=highest)
        spectral = from_grid(jnp.real(jnp.fft.ifftn(place_modes(mixed), axes=(1, 2, 3, 4))))
        local = jnp.einsum('xcn,co->xon', values, point_mat, precision=highest)
        pre = spectral + local + bias_vec[None, :, None]
        activated = jax.nn.gelu(pre, approximate=False).astype(jnp.bfloat16)
        upstream = sample_cot.astype(jnp.float32) * gelu_slope(pre)
        spec_up = select_modes(jnp.fft.fftn(to_grid(upstream), axes=(1, 2, 3, 4))) / volume
        back = jnp.einsum('com,om->cm', mixer_conj, spec_up, precision=highest)
        spectral_back = from_grid(jnp.real(jnp.fft.ifftn(place_modes(back), axes=(1, 2, 3, 4)))) * volume
        grad_in = (spectral_back + jnp.einsum('xon,co->xcn', upstream, point_mat, precision=highest)).astype(jnp.bfloat16)
        grad_term = jnp.conj(spec_in)[:, None, :] * spec_up[None, :, :]
        running = running + jnp.stack([jnp.real(grad_term), jnp.imag(grad_term)]).astype(jnp.float32)
        return (running, (activated, grad_in))
    initial = jnp.zeros((2, C, C, MZ * MT * MY * MX), jnp.float32)
    running, outputs = lax.scan(per_sample, initial, (fields, cotangent))
    return (outputs[0], outputs[1], running)
```

```python
import functools
import math

import jax
import jax.numpy as jnp
import numpy as np
from jax import lax
from jax.experimental import pallas as pl
from jax.experimental.pallas import tpu as pltpu
from jax.sharding import PartitionSpec as P

NX, NY, NZ, NT = 64, 64, 32, 4
MX, MY, MZ, MT = 12, 12, 8, 4
VOLUME = NX * NY * NZ * NT
PLANE = NZ * NT
XY = MX * MY
BF16, F32 = jnp.bfloat16, jnp.float32
VMEM_LIMIT = 60 * 1024 * 1024
GROUP = 4
MESH = pl.DeviceIdType.MESH


def signed(modes):
    index = np.arange(modes)
    return np.where(index < modes // 2, index, index - modes)


def split_np(table):
    high = table.astype(np.float32).astype(BF16)
    low = (table - high.astype(np.float64)).astype(np.float32).astype(BF16)
    return high, low


def tables(rows, space):
    fy, fx = signed(MY), signed(MX)
    y = np.arange(NY)
    x = np.arange(space * rows).reshape(space, rows)
    phi = 2 * np.pi * (
        (fy.reshape(1, MY, 1, 1, 1) * y.reshape(1, 1, 1, NY, 1) % NY) / NY
        + (fx.reshape(1, 1, MX, 1, 1) * x.reshape(space, 1, 1, 1, rows) % NX) / NX
    ).reshape(space, XY, NY * rows)
    plane = np.concatenate([np.cos(phi), np.sin(phi)], 1)
    hi, lo = split_np(plane)
    forward = np.concatenate([hi, lo], 1)
    turned = lambda t: np.transpose(t, (0, 2, 1))
    inverse = np.concatenate([turned(hi), turned(lo), turned(hi)], 2)
    fz, ft = signed(MZ), signed(MT)
    z, t = np.arange(NZ), np.arange(NT)
    psi = 2 * np.pi * (
        fz.reshape(MZ, 1, 1, 1) * z.reshape(1, 1, NZ, 1) / NZ
        + ft.reshape(1, MT, 1, 1) * t.reshape(1, 1, 1, NT) / NT
    ).reshape(space, MZ * MT // space, PLANE)
    cos, sin = np.cos(psi), np.sin(psi)
    depth = np.stack(
        [np.concatenate([cos, -sin], -1), np.concatenate([-sin, -cos], -1)], 1
    ).reshape(space, 2 * MZ * MT // space, 2 * PLANE)
    dhi, dlo = split_np(depth)
    flat = lambda t: t.reshape(2 * MZ * MT, 2 * PLANE)
    by_core = lambda t: flat(np.concatenate([t[0::2], t[1::2]], 0))
    depth_forward = np.concatenate([by_core(dhi), by_core(dlo)], 0)
    depth_inverse = np.concatenate([flat(dhi), flat(dhi), flat(dlo)], 0)
    return forward, inverse, depth_forward, depth_inverse


def split(value):
    high = value.astype(BF16)
    return high, (value - high.astype(F32)).astype(BF16)


def dot(a, b, contract=(1, 0)):
    dims = (((contract[0],), (contract[1],)), ((), ()))
    return lax.dot_general(a, b, dims, preferred_element_type=F32)


def forward_pair(block, fwd, zhi, zlo, p, exact):
    half = fwd.shape[0] // 2
    if exact:
        res = dot(fwd[...], block)
        res = res[:half] + res[half:]
    else:
        high, low = split(block)
        res = dot(fwd[...], high)
        res = res[:half] + res[half:] + dot(fwd[:half], low)
    for k in range(2):
        part = res[:, k * PLANE : (k + 1) * PLANE]
        high, low = split(jnp.concatenate([part[:XY], part[XY:]], -1))
        zhi[2 * p + k] = high
        zlo[2 * p + k] = low


def forward_depth(depth, zhi, zlo):
    rows = depth.shape[0] // 2
    high = zhi[...].reshape(-1, 2 * PLANE)
    low = zlo[...].reshape(-1, 2 * PLANE)
    first = dot(depth[...], high, (1, 1))
    return first[:rows] + first[rows:] + dot(depth[:rows], low, (1, 1))


def inverse_depth(modes, depth, grid):
    high, low = split(modes)
    stacked = jnp.concatenate([high, low, high], 0)
    lines = dot(stacked, depth[...], (0, 0)).reshape(GROUP, XY, 2 * PLANE)
    high, low = split(lines)
    for at, value in ((0, high), (2 * XY, high), (4 * XY, low)):
        grid[:, at : at + XY] = value[:, :, :PLANE]
        grid[:, at + XY : at + 2 * XY] = value[:, :, PLANE:]


def inverse_pair(inv, grid, p):
    return dot(inv[...], jnp.concatenate([grid[2 * p], grid[2 * p + 1]], -1))


def main_kernel(
    n, ns,
    fields_h, cot_h, weight_h, fwd_h, inv_h, depth_f, depth_i, point, bias_row, copies, copies_t, same,
    act_h, local_h, modes_h, spec_h, up_h,
    fields, cot, weight, fwd, inv, work, local, act, zhi, zlo, grid, pre, mix, mix_back, bias, pair_rows, w_re, w_im,
    part, near, joined, recv, modes, stage, lined, mixed, spec, got,
    load_sem, table_sem, act_sem, out_sem,
    near_send, near_recv, sum_send, sum_recv, all_send, all_recv, relay_send, relay_recv, side_send, side_recv,
):
    channels, cells, _ = fields.shape
    chunks = channels // GROUP
    rows = cells // NY
    flat = channels * rows
    chips = n // 2
    own_rows = stage.shape[1]
    owned = own_rows // 2
    per = ns // owned
    count = owned * XY // ns
    me = lax.axis_index("space")
    mine = lax.axis_index("sample")
    core = lax.rem(me, 2)
    chip = (me - core) // 2
    sibling = me + 1 - 2 * core

    barrier = pltpu.get_barrier_semaphore()
    for k in range(1, n):
        pl.semaphore_signal(barrier, inc=1, device_id={"space": lax.rem(me + k, n)}, device_id_type=MESH)
    for k in range(1, ns):
        pl.semaphore_signal(barrier, inc=1, device_id={"sample": lax.rem(mine + k, ns)}, device_id_type=MESH)

    def group(k):
        return pl.ds(k * GROUP, GROUP)

    def load(src, dst, which, k):
        return pltpu.make_async_copy(src.at[group(k)], dst.at[group(k)], load_sem.at[which, k])

    fwd_load = pltpu.make_async_copy(fwd_h.at[me], fwd, table_sem.at[0])
    inv_load = pltpu.make_async_copy(inv_h.at[me], inv, table_sem.at[1])
    weight_load = pltpu.make_async_copy(weight_h, weight, table_sem.at[2])
    fwd_load.start()
    for k in range(chunks):
        load(fields_h, fields, 0, k).start()
    weight_load.start()
    inv_load.start()
    for k in range(chunks):
        load(cot_h, cot, 1, k).start()

    def remote(src, dst, send, got_sem, axis, target):
        return pltpu.make_async_remote_copy(
            src_ref=src, dst_ref=dst, send_sem=send, recv_sem=got_sem,
            device_id={axis: target}, device_id_type=MESH,
        )

    def to_sibling(e, k):
        return remote(part.at[k, 1 - core], near.at[e, k], near_send.at[e, k], near_recv.at[e, k], "space", sibling)

    def to_owner(e, k, j):
        goal = lax.rem(chip + j, chips)
        return remote(
            joined.at[e, k, goal], recv.at[e, k, j - 1], sum_send.at[e, k, j], sum_recv.at[e, k, j], "space", 2 * goal + core
        )

    def to_all(e, k, j):
        target = lax.rem(me + 2 * j, n) if j else sibling
        return remote(modes.at[e, k, me], modes.at[e, k, me], all_send.at[e, k, j], all_recv.at[e, k, j], "space", target)

    def to_relay(e, k, j):
        block = modes.at[e, k, lax.rem(me + n - 2 * j, n)]
        return remote(block, block, relay_send.at[e, k, j], relay_recv.at[e, k, j], "space", sibling)

    def join(e, k):
        to_sibling(e, k).wait()
        total = part[k, core] + near[e, k]
        for j in range(chips):
            joined[e, k, j] = total[j * own_rows : (j + 1) * own_rows]
        for j in range(1, chips):
            to_owner(e, k, j).start()

    def put_part(k, value):
        half = value.shape[0] // 2
        part[k, 0] = value[:half]
        part[k, 1] = value[half:]

    def spread(matrix, side):
        half = dot(copies[...], matrix, (1, side)).astype(BF16)
        return dot(half, copies_t[...]).astype(BF16) * same[...]

    fwd_load.wait()
    pl.semaphore_wait(barrier, n - 1 + ns - 1)

    def first(k, carry):
        load(fields_h, fields, 0, k).wait()
        for p in range(GROUP // 2):
            c = k * GROUP + 2 * p
            forward_pair(jnp.concatenate([fields[c], fields[c + 1]], -1), fwd, zhi, zlo, p, True)
        put_part(k, forward_depth(depth_f, zhi, zlo))
        to_sibling(0, k).start()

        @pl.when(k > 0)
        def _():
            join(0, k - 1)

        return carry

    lax.fori_loop(0, chunks, first, 0)

    mix[...] = spread(point[...], 1)
    mix_back[...] = spread(point[...], 0)
    column = jnp.sum(copies[...].astype(F32) * bias_row[...], -1, keepdims=True)
    bias[...] = jnp.broadcast_to(column, (flat, PLANE))
    join(0, chunks - 1)

    weight_load.wait()

    def widen(c, carry):
        pair_rows[...] = weight[c].astype(F32)
        w_re[c] = pair_rows[:, 0, :]
        w_im[c] = pair_rows[:, 1, :]
        return carry

    lax.fori_loop(0, channels, widen, 0)

    def pointwise(i, carry):
        at = pl.multiple_of(i * 2 * rows, 2 * rows)
        block = fields[:, pl.ds(at, 2 * rows), :].astype(F32)
        block = jnp.concatenate([block[:, :rows], block[:, rows:]], -1).reshape(flat, 2 * PLANE)
        value = dot(mix[...], block.astype(BF16))
        for k in range(2):
            out = value[:, k * PLANE : (k + 1) * PLANE] + bias[...]
            work[:, pl.ds(pl.multiple_of(at + k * rows, rows), rows), :] = out.reshape(channels, rows, PLANE)
        return carry

    half_lines = NY // 4
    lax.fori_loop(0, half_lines, pointwise, 0, unroll=2)

    def gather_total(e, scale):
        for k in range(chunks):
            for j in range(1, chips):
                to_owner(e, k, j).wait()
            total = joined[e, k, chip]
            for j in range(1, chips):
                total = total + recv[e, k, j - 1]
            total = total * scale
            for g in range(GROUP):
                stage[g] = total[:, g * XY : (g + 1) * XY]
            for j in range(own_rows):
                r, q = j // owned, j % owned
                block = stage[:, j, :]
                lined[r, k * GROUP : (k + 1) * GROUP, q * XY : (q + 1) * XY] = block
                for p in range(per):
                    spec[e, q * per + p, r, k * GROUP : (k + 1) * GROUP] = block[:, p * count : (p + 1) * count]

    def side(e, j):
        goal = lax.rem(mine + j, ns)
        return remote(spec.at[e, goal], got.at[e, j], side_send.at[e, j], side_recv.at[e, j], "sample", goal)

    def scatter_mixed(e):
        for k in range(chunks):
            for j in range(own_rows):
                r, q = j // owned, j % owned
                stage[:, j, :] = mixed[r, k * GROUP : (k + 1) * GROUP, q * XY : (q + 1) * XY]
            modes[e, k, me] = jnp.concatenate([stage[g] for g in range(GROUP)], -1)
            for j in range(chips):
                to_all(e, k, j).start()

    gather_total(0, 1.0)

    def add(c, carry):
        w_r, w_i = w_re[c], w_im[c]
        s_r, s_i = lined[0, pl.ds(c, 1), :], lined[1, pl.ds(c, 1), :]
        return carry[0] + (w_r * s_r - w_i * s_i), carry[1] + (w_r * s_i + w_i * s_r)

    zero = jnp.zeros((channels, owned * XY), F32)
    real, imag = lax.fori_loop(0, channels, add, (zero, zero))
    mixed[0] = real * (1.0 / VOLUME)
    mixed[1] = imag * (1.0 / VOLUME)
    scatter_mixed(0)
    for j in range(1, ns):
        side(0, j).start()
    inv_load.wait()
    lax.fori_loop(half_lines, 2 * half_lines, pointwise, 0, unroll=2)

    def relay(e, k):
        for j in range(1, chips):
            to_all(e, k, j).wait()
            to_relay(e, k, j).start()

    def arrived(e, k):
        to_all(e, k, 0).wait()
        for j in range(1, chips):
            to_relay(e, k, j).wait()

    relay(0, 0)

    def act_store(k):
        return pltpu.make_async_copy(act.at[group(k)], act_h.at[group(k)], act_sem.at[k])

    def middle(k, carry):
        @pl.when(k + 1 < chunks)
        def _():
            relay(0, k + 1)

        arrived(0, k)
        inverse_depth(modes[0, k].reshape(n * own_rows, GROUP * XY), depth_i, grid)
        load(cot_h, cot, 1, k).wait()
        for p in range(GROUP // 2):
            pre[...] = inverse_pair(inv, grid, p)
            for h in range(2):
                c = k * GROUP + 2 * p + h
                value = pre[:, h * PLANE : (h + 1) * PLANE] + work[c]
                phi = 0.5 * (1.0 + lax.erf(value * (1.0 / math.sqrt(2.0))))
                slope = phi + value * jnp.exp(-0.5 * value * value) * (1.0 / math.sqrt(2.0 * math.pi))
                act[c] = (value * phi).astype(BF16)
                work[c] = cot[c].astype(F32) * slope
            c = k * GROUP + 2 * p
            forward_pair(jnp.concatenate([work[c], work[c + 1]], -1), fwd, zhi, zlo, p, False)
        act_store(k).start()

        put_part(k, forward_depth(depth_f, zhi, zlo))
        to_sibling(1, k).start()

        @pl.when(k > 0)
        def _():
            join(1, k - 1)

        return carry

    lax.fori_loop(0, chunks, middle, 0)

    def back(i, carry):
        at = pl.multiple_of(i * 2 * rows, 2 * rows)
        block = work[:, pl.ds(at, 2 * rows), :]
        block = jnp.concatenate([block[:, :rows], block[:, rows:]], -1).reshape(flat, 2 * PLANE)
        high, low = split(block)
        value = dot(mix_back[...], high) + dot(mix_back[...], low)
        for k in range(2):
            out = value[:, k * PLANE : (k + 1) * PLANE].reshape(channels, rows, PLANE)
            local[:, pl.ds(pl.multiple_of(at + k * rows, rows), rows), :] = out
        return carry

    lax.fori_loop(0, half_lines // 2, back, 0, unroll=2)
    join(1, chunks - 1)
    lax.fori_loop(half_lines // 2, 2 * half_lines, back, 0, unroll=2)
    local_store = pltpu.make_async_copy(local, local_h, out_sem.at[0])
    local_store.start()

    gather_total(1, 1.0 / VOLUME)
    for j in range(1, ns):
        side(1, j).start()

    def reduce(c, carry):
        w_r, w_i = w_re[c], w_im[c]
        u_r, u_i = lined[0], lined[1]
        mixed[0, pl.ds(c, 1), :] = jnp.sum(w_r * u_r + w_i * u_i, 0, keepdims=True)
        mixed[1, pl.ds(c, 1), :] = jnp.sum(w_r * u_i - w_i * u_r, 0, keepdims=True)
        return carry

    lax.fori_loop(0, channels, reduce, 0)
    scatter_mixed(1)

    for e in range(2):
        for j in range(1, ns):
            side(e, j).wait()
        got[e, 0] = spec[e, mine]
    spec_store = pltpu.make_async_copy(got.at[0], spec_h, out_sem.at[1])
    up_store = pltpu.make_async_copy(got.at[1], up_h, out_sem.at[2])
    spec_store.start()
    up_store.start()
    for k in range(chunks):
        relay(1, k)
    for k in range(chunks):
        arrived(1, k)
    modes_store = pltpu.make_async_copy(modes.at[1], modes_h, out_sem.at[3])
    modes_store.start()
    for k in range(chunks):
        act_store(k).wait()
    local_store.wait()
    spec_store.wait()
    up_store.wait()
    modes_store.wait()


def last_kernel(
    modes_h, local_h, spec_h, up_h, act_in, inv_h, depth_i,
    act_h, out_h, grad,
    modes, local, spec, up, act, inv, out, grid, load_sem, local_sem, act_sem, store_sem, pass_sem,
):
    channels = out.shape[0]
    chunks = channels // GROUP
    me = lax.axis_index("space")
    n = modes.shape[1]

    def group(k):
        return pl.ds(k * GROUP, GROUP)

    def local_load(k):
        return pltpu.make_async_copy(local_h.at[group(k)], local.at[group(k)], local_sem.at[k])

    def act_load(k):
        return pltpu.make_async_copy(act_in.at[group(k)], act.at[group(k)], act_sem.at[k])

    def act_store(k):
        return pltpu.make_async_copy(act.at[group(k)], act_h.at[group(k)], pass_sem.at[k])

    def out_store(k):
        return pltpu.make_async_copy(out.at[group(k)], out_h.at[group(k)], store_sem.at[k])

    first = [
        pltpu.make_async_copy(modes_h, modes, load_sem.at[0]),
        pltpu.make_async_copy(inv_h.at[me], inv, load_sem.at[1]),
        pltpu.make_async_copy(spec_h, spec, load_sem.at[2]),
        pltpu.make_async_copy(up_h, up, load_sem.at[3]),
    ]
    for copy in first:
        copy.start()
    for k in range(chunks):
        local_load(k).start()
        act_load(k).start()
    for copy in first:
        copy.wait()

    samples, _, _, count = spec.shape

    def chunk(k, carry):
        inverse_depth(modes[k].reshape(-1, GROUP * XY), depth_i, grid)
        local_load(k).wait()
        for p in range(GROUP // 2):
            res = inverse_pair(inv, grid, p)
            for h in range(2):
                c = k * GROUP + 2 * p + h
                out[c] = (res[:, h * PLANE : (h + 1) * PLANE] + local[c]).astype(BF16)
        out_store(k).start()
        act_load(k).wait()
        act_store(k).start()
        return carry

    lax.fori_loop(0, chunks, chunk, 0)

    def term(c, carry):
        real = jnp.zeros((channels, count), F32)
        imag = jnp.zeros((channels, count), F32)
        for s in range(samples):
            a_r, a_i = spec[s, 0, pl.ds(c, 1), :], spec[s, 1, pl.ds(c, 1), :]
            b_r, b_i = up[s, 0], up[s, 1]
            real = real + (a_r * b_r + a_i * b_i)
            imag = imag + (a_r * b_i - a_i * b_r)
        grad[c, :, 0, :] = real
        grad[c, :, 1, :] = imag
        return carry

    lax.fori_loop(0, channels, term, 0)
    for k in range(chunks):
        out_store(k).wait()
        act_store(k).wait()


def shards(fields, cotangent, spectral_weight, point_weight, point_bias):
    _, rows, channels, columns = fields.shape
    n = lax.axis_size("space")
    ns = lax.axis_size("sample")
    forward, inverse, depth_f, depth_i = [jnp.asarray(t) for t in tables(rows, n)]
    cells = NY * rows
    chunks = channels // GROUP
    chips = n // 2
    owned = MT * MZ // n
    own_rows = 2 * owned
    width = GROUP * XY
    flat = channels * rows
    count = owned * XY // ns
    copies = np.repeat(np.eye(channels), rows, 0).astype(BF16)
    same = np.tile(np.eye(rows), (channels, channels)).astype(BF16)

    def by_channel(value):
        value = value[0].reshape(rows, channels, NY, PLANE)
        return jnp.transpose(value, (1, 2, 0, 3)).reshape(channels, cells, PLANE)

    def by_row(value):
        value = jnp.transpose(value.reshape(channels, NY, rows, PLANE), (2, 0, 1, 3))
        return value.reshape(1, rows, channels, columns)

    weight = jnp.transpose(spectral_weight, (1, 2, 0, 3))
    vmem, dma = pltpu.VMEM, pltpu.SemaphoreType.DMA
    any_spec, vmem_spec = pl.BlockSpec(memory_space=pl.ANY), pl.BlockSpec(memory_space=vmem)
    shape = jax.ShapeDtypeStruct
    kept = (ns, 2, channels, count)
    grid_bf = shape((channels, cells, PLANE), BF16)
    grid_f = shape((channels, cells, PLANE), F32)
    modes_shape = (chunks, n, own_rows, width)

    act, local, modes, spec, up = pl.pallas_call(
        functools.partial(main_kernel, n, ns),
        out_shape=[grid_bf, grid_f, shape(modes_shape, F32), shape(kept, F32), shape(kept, F32)],
        in_specs=[any_spec] * 5 + [vmem_spec] * 7,
        out_specs=[any_spec] * 5,
        scratch_shapes=[
            vmem((channels, cells, PLANE), BF16),
            vmem((channels, cells, PLANE), BF16),
            vmem(weight.shape, BF16),
            vmem(forward.shape[1:], BF16),
            vmem(inverse.shape[1:], BF16),
            vmem((channels, cells, PLANE), F32),
            vmem((channels, cells, PLANE), F32),
            vmem((channels, cells, PLANE), BF16),
            vmem((GROUP, XY, 2 * PLANE), BF16),
            vmem((GROUP, XY, 2 * PLANE), BF16),
            vmem((GROUP, 6 * XY, PLANE), BF16),
            vmem((cells, 2 * PLANE), F32),
            vmem((flat, flat), BF16),
            vmem((flat, flat), BF16),
            vmem((flat, PLANE), F32),
            vmem((channels, 2, owned * XY), F32),
            vmem((channels, channels, owned * XY), F32),
            vmem((channels, channels, owned * XY), F32),
            vmem((chunks, 2, chips * own_rows, width), F32),
            vmem((2, chunks, chips * own_rows, width), F32),
            vmem((2, chunks, chips, own_rows, width), F32),
            vmem((2, chunks, chips - 1, own_rows, width), F32),
            vmem((2,) + modes_shape, F32),
            vmem((GROUP, own_rows, XY), F32),
            vmem((2, channels, owned * XY), F32),
            vmem((2, channels, owned * XY), F32),
            vmem((2,) + kept, F32),
            vmem((2,) + kept, F32),
            dma((2, chunks)), dma((3,)), dma((chunks,)), dma((4,)),
            dma((2, chunks)), dma((2, chunks)),
            dma((2, chunks, chips)), dma((2, chunks, chips)),
            dma((2, chunks, chips)), dma((2, chunks, chips)),
            dma((2, chunks, chips)), dma((2, chunks, chips)),
            dma((2, ns)), dma((2, ns)),
        ],
        compiler_params=pltpu.CompilerParams(
            vmem_limit_bytes=VMEM_LIMIT, collective_id=0, has_side_effects=True
        ),
    )(
        by_channel(fields), by_channel(cotangent), weight, forward, inverse, depth_f, depth_i,
        point_weight, point_bias[None], copies, copies.T, same,
    )

    act_out, grad_in, grad = pl.pallas_call(
        last_kernel,
        out_shape=[grid_bf, grid_bf, shape((channels, channels, 2, count), F32)],
        in_specs=[any_spec] * 6 + [vmem_spec],
        out_specs=[any_spec, any_spec, vmem_spec],
        scratch_shapes=[
            vmem(modes_shape, F32),
            vmem((channels, cells, PLANE), F32),
            vmem(kept, F32),
            vmem(kept, F32),
            vmem((channels, cells, PLANE), BF16),
            vmem(inverse.shape[1:], BF16),
            vmem((channels, cells, PLANE), BF16),
            vmem((GROUP, 6 * XY, PLANE), BF16),
            dma((4,)), dma((chunks,)), dma((chunks,)), dma((chunks,)), dma((chunks,)),
        ],
        compiler_params=pltpu.CompilerParams(vmem_limit_bytes=VMEM_LIMIT),
    )(modes, local, spec, up, act, inverse, depth_i)
    return by_row(act_out), by_row(grad_in), jnp.transpose(grad, (2, 0, 1, 3))


def solution(mesh):
    return jax.shard_map(
        shards,
        mesh=mesh,
        in_specs=(
            P("sample", "space", None, None),
            P("sample", "space", None, None),
            P(None, None, None, "space"),
            P(),
            P(),
        ),
        out_specs=(
            P("sample", "space", None, None),
            P("sample", "space", None, None),
            P(None, None, None, ("space", "sample")),
        ),
        check_vma=False,
    )
```

```python
import functools
import math

import jax
import jax.numpy as jnp
import numpy as np
from jax import lax
from jax.experimental import pallas as pl
from jax.experimental.pallas import tpu as pltpu
from jax.sharding import PartitionSpec as P

NX, NY, NZ, NT = 64, 64, 32, 4
MX, MY, MZ, MT = 12, 12, 8, 4
VOLUME = NX * NY * NZ * NT
PLANE = NZ * NT
XY = MX * MY
BF16, F32 = jnp.bfloat16, jnp.float32
VMEM_LIMIT = 44 * 1024 * 1024
GROUP = 4
MESH = pl.DeviceIdType.MESH


def signed(modes):
    index = np.arange(modes)
    return np.where(index < modes // 2, index, index - modes)


def split_np(table):
    high = table.astype(np.float32).astype(BF16)
    low = (table - high.astype(np.float64)).astype(np.float32).astype(BF16)
    return high, low


def tables(rows, space):
    fy, fx = signed(MY), signed(MX)
    y = np.arange(NY)
    x = np.arange(space * rows).reshape(space, rows)
    phi = 2 * np.pi * (
        (fy.reshape(1, MY, 1, 1, 1) * y.reshape(1, 1, 1, NY, 1) % NY) / NY
        + (fx.reshape(1, 1, MX, 1, 1) * x.reshape(space, 1, 1, 1, rows) % NX) / NX
    ).reshape(space, XY, NY * rows)
    plane = np.concatenate([np.cos(phi), np.sin(phi)], 1)
    hi, lo = split_np(plane)
    forward = np.concatenate([hi, lo], 1)
    turned = lambda t: np.transpose(t, (0, 2, 1))
    inverse = np.concatenate([turned(hi), turned(lo), turned(hi)], 2)
    fz, ft = signed(MZ), signed(MT)
    z, t = np.arange(NZ), np.arange(NT)
    psi = 2 * np.pi * (
        fz.reshape(MZ, 1, 1, 1) * z.reshape(1, 1, NZ, 1) / NZ
        + ft.reshape(1, MT, 1, 1) * t.reshape(1, 1, 1, NT) / NT
    ).reshape(space, MZ * MT // space, PLANE)
    cos, sin = np.cos(psi), np.sin(psi)
    depth = np.stack(
        [np.concatenate([cos, -sin], -1), np.concatenate([-sin, -cos], -1)], 1
    ).reshape(space, 2 * MZ * MT // space, 2 * PLANE)
    dhi, dlo = split_np(depth)
    flat = lambda t: t.reshape(2 * MZ * MT, 2 * PLANE)
    by_core = lambda t: flat(np.concatenate([t[0::2], t[1::2]], 0))
    depth_forward = np.concatenate([by_core(dhi), by_core(dlo)], 0)
    depth_inverse = np.concatenate([flat(dhi), flat(dhi), flat(dlo)], 0)
    return forward, inverse, depth_forward, depth_inverse


def split(value):
    high = value.astype(BF16)
    return high, (value - high.astype(F32)).astype(BF16)


def dot(a, b, contract=(1, 0)):
    dims = (((contract[0],), (contract[1],)), ((), ()))
    return lax.dot_general(a, b, dims, preferred_element_type=F32)


def forward_pair(block, fwd, zhi, zlo, p, exact):
    half = fwd.shape[0] // 2
    if exact:
        res = dot(fwd[...], block)
        res = res[:half] + res[half:]
    else:
        high, low = split(block)
        res = dot(fwd[...], high)
        res = res[:half] + res[half:] + dot(fwd[:half], low)
    for k in range(2):
        part = res[:, k * PLANE : (k + 1) * PLANE]
        high, low = split(jnp.concatenate([part[:XY], part[XY:]], -1))
        zhi[2 * p + k] = high
        zlo[2 * p + k] = low


def forward_depth(depth, zhi, zlo):
    rows = depth.shape[0] // 2
    high = zhi[...].reshape(-1, 2 * PLANE)
    low = zlo[...].reshape(-1, 2 * PLANE)
    first = dot(depth[...], high, (1, 1))
    return first[:rows] + first[rows:] + dot(depth[:rows], low, (1, 1))


def inverse_depth(modes, depth, grid):
    high, low = split(modes)
    stacked = jnp.concatenate([high, low, high], 0)
    lines = dot(stacked, depth[...], (0, 0)).reshape(GROUP, XY, 2 * PLANE)
    high, low = split(lines)
    for at, value in ((0, high), (2 * XY, high), (4 * XY, low)):
        grid[:, at : at + XY] = value[:, :, :PLANE]
        grid[:, at + XY : at + 2 * XY] = value[:, :, PLANE:]


def inverse_pair(inv, grid, p):
    return dot(inv[...], jnp.concatenate([grid[2 * p], grid[2 * p + 1]], -1))


def main_kernel(
    n, ns,
    fields_h, cot_h, weight_h, fwd_h, inv_h, depth_f, depth_i, point, bias_row, copies, copies_t, same,
    act, out, grad,
    fields, cot, weight, fwd, inv, work, local, zhi, zlo, grid, pre, mix, mix_back, bias, pair_rows, w_re, w_im,
    part, near, joined, recv, modes, stage, lined, mixed, spec, got,
    load_sem, table_sem,
    near_send, near_recv, sum_send, sum_recv, all_send, all_recv, relay_send, relay_recv, side_send, side_recv,
):
    channels, cells, _ = fields.shape
    chunks = channels // GROUP
    rows = cells // NY
    flat = channels * rows
    chips = n // 2
    own_rows = stage.shape[1]
    owned = own_rows // 2
    per = ns // owned
    count = owned * XY // ns
    me = lax.axis_index("space")
    mine = lax.axis_index("sample")
    core = lax.rem(me, 2)
    chip = (me - core) // 2
    sibling = me + 1 - 2 * core

    barrier = pltpu.get_barrier_semaphore()
    for k in range(1, n):
        pl.semaphore_signal(barrier, inc=1, device_id={"space": lax.rem(me + k, n)}, device_id_type=MESH)
    for k in range(1, ns):
        pl.semaphore_signal(barrier, inc=1, device_id={"sample": lax.rem(mine + k, ns)}, device_id_type=MESH)

    def group(k):
        return pl.ds(k * GROUP, GROUP)

    def load(src, dst, which, k):
        return pltpu.make_async_copy(src.at[group(k)], dst.at[group(k)], load_sem.at[which, k])

    fwd_load = pltpu.make_async_copy(fwd_h.at[me], fwd, table_sem.at[0])
    inv_load = pltpu.make_async_copy(inv_h.at[me], inv, table_sem.at[1])
    weight_load = pltpu.make_async_copy(weight_h, weight, table_sem.at[2])
    fwd_load.start()
    for k in range(chunks):
        load(fields_h, fields, 0, k).start()
    weight_load.start()
    inv_load.start()
    for k in range(chunks):
        load(cot_h, cot, 1, k).start()

    def remote(src, dst, send, got_sem, axis, target):
        return pltpu.make_async_remote_copy(
            src_ref=src, dst_ref=dst, send_sem=send, recv_sem=got_sem,
            device_id={axis: target}, device_id_type=MESH,
        )

    def to_sibling(e, k):
        return remote(part.at[k, 1 - core], near.at[e, k], near_send.at[e, k], near_recv.at[e, k], "space", sibling)

    def to_owner(e, k, j):
        goal = lax.rem(chip + j, chips)
        return remote(
            joined.at[e, k, goal], recv.at[e, k, j - 1], sum_send.at[e, k, j], sum_recv.at[e, k, j], "space", 2 * goal + core
        )

    def to_all(e, k, j):
        target = lax.rem(me + 2 * j, n) if j else sibling
        return remote(modes.at[e, k, me], modes.at[e, k, me], all_send.at[e, k, j], all_recv.at[e, k, j], "space", target)

    def to_relay(e, k, j):
        block = modes.at[e, k, lax.rem(me + n - 2 * j, n)]
        return remote(block, block, relay_send.at[e, k, j], relay_recv.at[e, k, j], "space", sibling)

    def join(e, k):
        to_sibling(e, k).wait()
        total = part[k, core] + near[e, k]
        for j in range(chips):
            joined[e, k, j] = total[j * own_rows : (j + 1) * own_rows]
        for j in range(1, chips):
            to_owner(e, k, j).start()

    def put_part(k, value):
        half = value.shape[0] // 2
        part[k, 0] = value[:half]
        part[k, 1] = value[half:]

    def spread(matrix, side):
        half = dot(copies[...], matrix, (1, side)).astype(BF16)
        return dot(half, copies_t[...]).astype(BF16) * same[...]

    fwd_load.wait()
    pl.semaphore_wait(barrier, n - 1 + ns - 1)

    def first(k, carry):
        load(fields_h, fields, 0, k).wait()
        for p in range(GROUP // 2):
            c = k * GROUP + 2 * p
            forward_pair(jnp.concatenate([fields[c], fields[c + 1]], -1), fwd, zhi, zlo, p, True)
        put_part(k, forward_depth(depth_f, zhi, zlo))
        to_sibling(0, k).start()

        @pl.when(k > 0)
        def _():
            join(0, k - 1)

        return carry

    lax.fori_loop(0, chunks, first, 0)

    mix[...] = spread(point[...], 1)
    mix_back[...] = spread(point[...], 0)
    column = jnp.sum(copies[...].astype(F32) * bias_row[...], -1, keepdims=True)
    bias[...] = jnp.broadcast_to(column, (flat, PLANE))
    join(0, chunks - 1)

    weight_load.wait()

    def widen(c, carry):
        pair_rows[...] = weight[c].astype(F32)
        w_re[c] = pair_rows[:, 0, :]
        w_im[c] = pair_rows[:, 1, :]
        return carry

    lax.fori_loop(0, channels, widen, 0)

    def pointwise(i, carry):
        at = pl.multiple_of(i * 2 * rows, 2 * rows)
        block = fields[:, pl.ds(at, 2 * rows), :].astype(F32)
        block = jnp.concatenate([block[:, :rows], block[:, rows:]], -1).reshape(flat, 2 * PLANE)
        value = dot(mix[...], block.astype(BF16))
        for k in range(2):
            out = value[:, k * PLANE : (k + 1) * PLANE] + bias[...]
            work[:, pl.ds(pl.multiple_of(at + k * rows, rows), rows), :] = out.reshape(channels, rows, PLANE)
        return carry

    half_lines = NY // 4
    lax.fori_loop(0, half_lines, pointwise, 0, unroll=2)

    def gather_total(e, scale):
        for k in range(chunks):
            for j in range(1, chips):
                to_owner(e, k, j).wait()
            total = joined[e, k, chip]
            for j in range(1, chips):
                total = total + recv[e, k, j - 1]
            total = total * scale
            for g in range(GROUP):
                stage[g] = total[:, g * XY : (g + 1) * XY]
            for j in range(own_rows):
                r, q = j // owned, j % owned
                block = stage[:, j, :]
                lined[r, k * GROUP : (k + 1) * GROUP, q * XY : (q + 1) * XY] = block
                for p in range(per):
                    spec[e, q * per + p, r, k * GROUP : (k + 1) * GROUP] = block[:, p * count : (p + 1) * count]

    def side(e, j):
        goal = lax.rem(mine + j, ns)
        return remote(spec.at[e, goal], got.at[e, j], side_send.at[e, j], side_recv.at[e, j], "sample", goal)

    def scatter_mixed(e):
        for k in range(chunks):
            for j in range(own_rows):
                r, q = j // owned, j % owned
                stage[:, j, :] = mixed[r, k * GROUP : (k + 1) * GROUP, q * XY : (q + 1) * XY]
            modes[e, k, me] = jnp.concatenate([stage[g] for g in range(GROUP)], -1)
            for j in range(chips):
                to_all(e, k, j).start()

    gather_total(0, 1.0)

    def add(c, carry):
        w_r, w_i = w_re[c], w_im[c]
        s_r, s_i = lined[0, pl.ds(c, 1), :], lined[1, pl.ds(c, 1), :]
        return carry[0] + (w_r * s_r - w_i * s_i), carry[1] + (w_r * s_i + w_i * s_r)

    zero = jnp.zeros((channels, owned * XY), F32)
    real, imag = lax.fori_loop(0, channels, add, (zero, zero))
    mixed[0] = real * (1.0 / VOLUME)
    mixed[1] = imag * (1.0 / VOLUME)
    scatter_mixed(0)
    for j in range(1, ns):
        side(0, j).start()
    inv_load.wait()
    lax.fori_loop(half_lines, 2 * half_lines, pointwise, 0, unroll=2)

    def relay(e, k):
        for j in range(1, chips):
            to_all(e, k, j).wait()
            to_relay(e, k, j).start()

    def arrived(e, k):
        to_all(e, k, 0).wait()
        for j in range(1, chips):
            to_relay(e, k, j).wait()

    relay(0, 0)

    def middle(k, carry):
        @pl.when(k + 1 < chunks)
        def _():
            relay(0, k + 1)

        arrived(0, k)
        inverse_depth(modes[0, k].reshape(n * own_rows, GROUP * XY), depth_i, grid)
        load(cot_h, cot, 1, k).wait()
        for p in range(GROUP // 2):
            pre[...] = inverse_pair(inv, grid, p)
            for h in range(2):
                c = k * GROUP + 2 * p + h
                value = pre[:, h * PLANE : (h + 1) * PLANE] + work[c]
                phi = 0.5 * (1.0 + lax.erf(value * (1.0 / math.sqrt(2.0))))
                slope = phi + value * jnp.exp(-0.5 * value * value) * (1.0 / math.sqrt(2.0 * math.pi))
                act[c] = (value * phi).astype(BF16)
                work[c] = cot[c].astype(F32) * slope
            c = k * GROUP + 2 * p
            forward_pair(jnp.concatenate([work[c], work[c + 1]], -1), fwd, zhi, zlo, p, False)

        put_part(k, forward_depth(depth_f, zhi, zlo))
        to_sibling(1, k).start()

        @pl.when(k > 0)
        def _():
            join(1, k - 1)

        return carry

    lax.fori_loop(0, chunks, middle, 0)

    def back(i, carry):
        at = pl.multiple_of(i * 2 * rows, 2 * rows)
        block = work[:, pl.ds(at, 2 * rows), :]
        block = jnp.concatenate([block[:, :rows], block[:, rows:]], -1).reshape(flat, 2 * PLANE)
        high, low = split(block)
        value = dot(mix_back[...], high) + dot(mix_back[...], low)
        for k in range(2):
            out = value[:, k * PLANE : (k + 1) * PLANE].reshape(channels, rows, PLANE)
            local[:, pl.ds(pl.multiple_of(at + k * rows, rows), rows), :] = out
        return carry

    lax.fori_loop(0, half_lines // 2, back, 0, unroll=2)
    join(1, chunks - 1)
    lax.fori_loop(half_lines // 2, 2 * half_lines, back, 0, unroll=2)

    gather_total(1, 1.0 / VOLUME)
    for j in range(1, ns):
        side(1, j).start()

    def reduce(c, carry):
        w_r, w_i = w_re[c], w_im[c]
        u_r, u_i = lined[0], lined[1]
        mixed[0, pl.ds(c, 1), :] = jnp.sum(w_r * u_r + w_i * u_i, 0, keepdims=True)
        mixed[1, pl.ds(c, 1), :] = jnp.sum(w_r * u_i - w_i * u_r, 0, keepdims=True)
        return carry

    lax.fori_loop(0, channels, reduce, 0)
    scatter_mixed(1)
    relay(1, 0)

    for e in range(2):
        for j in range(1, ns):
            side(e, j).wait()
        got[e, 0] = spec[e, mine]

    def term(c, carry):
        real = jnp.zeros((channels, count), F32)
        imag = jnp.zeros((channels, count), F32)
        for s in range(ns):
            a_r, a_i = got[0, s, 0, pl.ds(c, 1), :], got[0, s, 1, pl.ds(c, 1), :]
            b_r, b_i = got[1, s, 0], got[1, s, 1]
            real = real + (a_r * b_r + a_i * b_i)
            imag = imag + (a_r * b_i - a_i * b_r)
        grad[c, :, 0, :] = real
        grad[c, :, 1, :] = imag
        return carry

    lax.fori_loop(0, channels, term, 0)

    def last(k, carry):
        @pl.when(k + 1 < chunks)
        def _():
            relay(1, k + 1)

        arrived(1, k)
        inverse_depth(modes[1, k].reshape(n * own_rows, GROUP * XY), depth_i, grid)
        for p in range(GROUP // 2):
            res = inverse_pair(inv, grid, p)
            for h in range(2):
                c = k * GROUP + 2 * p + h
                out[c] = (res[:, h * PLANE : (h + 1) * PLANE] + local[c]).astype(BF16)
        return carry

    lax.fori_loop(0, chunks, last, 0)


def shards(fields, cotangent, spectral_weight, point_weight, point_bias):
    _, rows, channels, columns = fields.shape
    n = lax.axis_size("space")
    ns = lax.axis_size("sample")
    forward, inverse, depth_f, depth_i = [jnp.asarray(t) for t in tables(rows, n)]
    cells = NY * rows
    chunks = channels // GROUP
    chips = n // 2
    owned = MT * MZ // n
    own_rows = 2 * owned
    width = GROUP * XY
    flat = channels * rows
    count = owned * XY // ns
    copies = np.repeat(np.eye(channels), rows, 0).astype(BF16)
    same = np.tile(np.eye(rows), (channels, channels)).astype(BF16)

    def by_channel(value):
        value = value[0].reshape(rows, channels, NY, PLANE)
        return jnp.transpose(value, (1, 2, 0, 3)).reshape(channels, cells, PLANE)

    def by_row(value):
        value = jnp.transpose(value.reshape(channels, NY, rows, PLANE), (2, 0, 1, 3))
        return value.reshape(1, rows, channels, columns)

    weight = jnp.transpose(spectral_weight, (1, 2, 0, 3))
    vmem, dma = pltpu.VMEM, pltpu.SemaphoreType.DMA
    any_spec, vmem_spec = pl.BlockSpec(memory_space=pltpu.HBM), pl.BlockSpec(memory_space=vmem)
    kept = (ns, 2, channels, count)
    modes_shape = (chunks, n, own_rows, width)

    act, grad_in, grad = pl.pallas_call(
        functools.partial(main_kernel, n, ns),
        out_shape=[
            vmem((channels, cells, PLANE), BF16),
            vmem((channels, cells, PLANE), BF16),
            vmem((channels, channels, 2, count), F32),
        ],
        in_specs=[any_spec] * 5 + [vmem_spec] * 7,
        out_specs=[vmem_spec] * 3,
        scratch_shapes=[
            vmem((channels, cells, PLANE), BF16),
            vmem((channels, cells, PLANE), BF16),
            vmem(weight.shape, BF16),
            vmem(forward.shape[1:], BF16),
            vmem(inverse.shape[1:], BF16),
            vmem((channels, cells, PLANE), F32),
            vmem((channels, cells, PLANE), F32),
            vmem((GROUP, XY, 2 * PLANE), BF16),
            vmem((GROUP, XY, 2 * PLANE), BF16),
            vmem((GROUP, 6 * XY, PLANE), BF16),
            vmem((cells, 2 * PLANE), F32),
            vmem((flat, flat), BF16),
            vmem((flat, flat), BF16),
            vmem((flat, PLANE), F32),
            vmem((channels, 2, owned * XY), F32),
            vmem((channels, channels, owned * XY), F32),
            vmem((channels, channels, owned * XY), F32),
            vmem((chunks, 2, chips * own_rows, width), F32),
            vmem((2, chunks, chips * own_rows, width), F32),
            vmem((2, chunks, chips, own_rows, width), F32),
            vmem((2, chunks, chips - 1, own_rows, width), F32),
            vmem((2,) + modes_shape, F32),
            vmem((GROUP, own_rows, XY), F32),
            vmem((2, channels, owned * XY), F32),
            vmem((2, channels, owned * XY), F32),
            vmem((2,) + kept, F32),
            vmem((2,) + kept, F32),
            dma((2, chunks)), dma((3,)),
            dma((2, chunks)), dma((2, chunks)),
            dma((2, chunks, chips)), dma((2, chunks, chips)),
            dma((2, chunks, chips)), dma((2, chunks, chips)),
            dma((2, chunks, chips)), dma((2, chunks, chips)),
            dma((2, ns)), dma((2, ns)),
        ],
        compiler_params=pltpu.CompilerParams(
            vmem_limit_bytes=VMEM_LIMIT, collective_id=0, has_side_effects=True
        ),
    )(
        by_channel(fields), by_channel(cotangent), weight, forward, inverse, depth_f, depth_i,
        point_weight, point_bias[None], copies, copies.T, same,
    )

    return by_row(act), by_row(grad_in), jnp.transpose(grad, (2, 0, 1, 3))


def solution(mesh):
    return jax.shard_map(
        shards,
        mesh=mesh,
        in_specs=(
            P("sample", "space", None, None),
            P("sample", "space", None, None),
            P(None, None, None, "space"),
            P(),
            P(),
        ),
        out_specs=(
            P("sample", "space", None, None),
            P("sample", "space", None, None),
            P(None, None, None, ("space", "sample")),
        ),
        check_vma=False,
    )
```

```python
import functools
import math

import jax
import jax.numpy as jnp
import numpy as np
from jax import lax
from jax.experimental import pallas as pl
from jax.experimental.pallas import tpu as pltpu
from jax.sharding import PartitionSpec as P

NX, NY, NZ, NT = 64, 64, 32, 4
MX, MY, MZ, MT = 12, 12, 8, 4
VOLUME = NX * NY * NZ * NT
PLANE = NZ * NT
XY = MX * MY
BF16, F32 = jnp.bfloat16, jnp.float32
VMEM_LIMIT = 60_970_000
GROUP = 4
MESH = pl.DeviceIdType.MESH


def signed(modes):
    index = np.arange(modes)
    return np.where(index < modes // 2, index, index - modes)


def split_np(table):
    high = table.astype(np.float32).astype(BF16)
    low = (table - high.astype(np.float64)).astype(np.float32).astype(BF16)
    return high, low


def tables(rows, space):
    fy, fx = signed(MY), signed(MX)
    y = np.arange(NY)
    x = np.arange(space * rows).reshape(space, rows)
    phi = 2 * np.pi * (
        (fy.reshape(1, MY, 1, 1, 1) * y.reshape(1, 1, 1, NY, 1) % NY) / NY
        + (fx.reshape(1, 1, MX, 1, 1) * x.reshape(space, 1, 1, 1, rows) % NX) / NX
    ).reshape(space, XY, NY * rows)
    plane = np.concatenate([np.cos(phi), np.sin(phi)], 1)
    hi, lo = split_np(plane)
    forward = np.concatenate([hi, lo], 1)
    turned = lambda t: np.transpose(t, (0, 2, 1))
    inverse = np.concatenate([turned(hi), turned(lo), turned(hi)], 2)
    fz, ft = signed(MZ), signed(MT)
    z, t = np.arange(NZ), np.arange(NT)
    psi = 2 * np.pi * (
        fz.reshape(MZ, 1, 1, 1) * z.reshape(1, 1, NZ, 1) / NZ
        + ft.reshape(1, MT, 1, 1) * t.reshape(1, 1, 1, NT) / NT
    ).reshape(space, MZ * MT // space, PLANE)
    cos, sin = np.cos(psi), np.sin(psi)
    depth = np.stack(
        [np.concatenate([cos, -sin], -1), np.concatenate([-sin, -cos], -1)], 1
    ).reshape(space, 2 * MZ * MT // space, 2 * PLANE)
    dhi, dlo = split_np(depth)
    flat = lambda t: t.reshape(2 * MZ * MT, 2 * PLANE)
    by_core = lambda t: flat(np.concatenate([t[0::2], t[1::2]], 0))
    depth_forward = np.concatenate([by_core(dhi), by_core(dlo)], 0)
    depth_inverse = np.concatenate([flat(dhi), flat(dhi), flat(dlo)], 0)
    return forward, inverse, depth_forward, depth_inverse


def split(value):
    high = value.astype(BF16)
    return high, (value - high.astype(F32)).astype(BF16)


def dot(a, b, contract=(1, 0)):
    dims = (((contract[0],), (contract[1],)), ((), ()))
    return lax.dot_general(a, b, dims, preferred_element_type=F32)


def forward_pair(block, fwd, zhi, zlo, p, exact):
    half = fwd.shape[0] // 2
    if exact:
        res = dot(fwd[...], block)
        res = res[:half] + res[half:]
    else:
        high, low = split(block)
        res = dot(fwd[...], high)
        res = res[:half] + res[half:] + dot(fwd[:half], low)
    for k in range(2):
        part = res[:, k * PLANE : (k + 1) * PLANE]
        high, low = split(jnp.concatenate([part[:XY], part[XY:]], -1))
        zhi[2 * p + k] = high
        zlo[2 * p + k] = low


def forward_depth(depth, zhi, zlo):
    rows = depth.shape[0] // 2
    high = zhi[...].reshape(-1, 2 * PLANE)
    low = zlo[...].reshape(-1, 2 * PLANE)
    first = dot(depth[...], high, (1, 1))
    return first[:rows] + first[rows:] + dot(depth[:rows], low, (1, 1))


def inverse_depth(modes, depth, grid):
    high, low = split(modes)
    stacked = jnp.concatenate([high, low, high], 0)
    lines = dot(stacked, depth[...], (0, 0)).reshape(GROUP, XY, 2 * PLANE)
    high, low = split(lines)
    for at, value in ((0, high), (2 * XY, high), (4 * XY, low)):
        grid[:, at : at + XY] = value[:, :, :PLANE]
        grid[:, at + XY : at + 2 * XY] = value[:, :, PLANE:]


def inverse_pair(inv, grid, p):
    return dot(inv[...], jnp.concatenate([grid[2 * p], grid[2 * p + 1]], -1))


def main_kernel(
    n, ns,
    fields_h, cot_h, weight_h, fwd_h, inv_h, depth_f, depth_i, point, bias_row, copies, copies_t, same,
    act, out, grad,
    fields, cot, weight, fwd, inv, work, local, zhi, zlo, grid, pre, mix, mix_back, bias, pair_rows, w_re, w_im,
    part, near, joined, recv, modes, stage, lined, mixed, spec, got,
    load_sem, table_sem,
    near_send, near_recv, sum_send, sum_recv, all_send, all_recv, relay_send, relay_recv, side_send, side_recv,
):
    channels, cells, _ = fields.shape
    chunks = channels // GROUP
    rows = cells // NY
    flat = channels * rows
    chips = n // 2
    own_rows = stage.shape[1]
    owned = own_rows // 2
    per = ns // owned
    count = owned * XY // ns
    me = lax.axis_index("space")
    mine = lax.axis_index("sample")
    core = lax.rem(me, 2)
    chip = (me - core) // 2
    sibling = me + 1 - 2 * core

    barrier = pltpu.get_barrier_semaphore()
    for k in range(1, n):
        pl.semaphore_signal(barrier, inc=1, device_id={"space": lax.rem(me + k, n)}, device_id_type=MESH)
    for k in range(1, ns):
        pl.semaphore_signal(barrier, inc=1, device_id={"sample": lax.rem(mine + k, ns)}, device_id_type=MESH)

    def group(k):
        return pl.ds(k * GROUP, GROUP)

    def load(src, dst, which, k):
        return pltpu.make_async_copy(src.at[group(k)], dst.at[group(k)], load_sem.at[which, k])

    fwd_load = pltpu.make_async_copy(fwd_h.at[me], fwd, table_sem.at[0])
    inv_load = pltpu.make_async_copy(inv_h.at[me], inv, table_sem.at[1])
    weight_load = pltpu.make_async_copy(weight_h, weight, table_sem.at[2])
    fwd_load.start()
    for k in range(chunks):
        load(fields_h, fields, 0, k).start()
    weight_load.start()
    inv_load.start()
    for k in range(chunks):
        load(cot_h, cot, 1, k).start()

    def remote(src, dst, send, got_sem, axis, target):
        return pltpu.make_async_remote_copy(
            src_ref=src, dst_ref=dst, send_sem=send, recv_sem=got_sem,
            device_id={axis: target}, device_id_type=MESH,
        )

    def to_sibling(e, k):
        return remote(part.at[k, 1 - core], near.at[e, k], near_send.at[e, k], near_recv.at[e, k], "space", sibling)

    def to_owner(e, k, j):
        goal = lax.rem(chip + j, chips)
        return remote(
            joined.at[e, k, goal], recv.at[e, k, j - 1], sum_send.at[e, k, j], sum_recv.at[e, k, j], "space", 2 * goal + core
        )

    def to_all(e, k, j):
        target = lax.rem(me + 2 * j, n) if j else sibling
        return remote(modes.at[e, k, me], modes.at[e, k, me], all_send.at[e, k, j], all_recv.at[e, k, j], "space", target)

    def to_relay(e, k, j):
        block = modes.at[e, k, lax.rem(me + n - 2 * j, n)]
        return remote(block, block, relay_send.at[e, k, j], relay_recv.at[e, k, j], "space", sibling)

    def join(e, k):
        to_sibling(e, k).wait()
        total = part[k, core] + near[e, k]
        for j in range(chips):
            joined[e, k, j] = total[j * own_rows : (j + 1) * own_rows]
        for j in range(1, chips):
            to_owner(e, k, j).start()

    def put_part(k, value):
        half = value.shape[0] // 2
        part[k, 0] = value[:half]
        part[k, 1] = value[half:]

    def spread(matrix, side):
        half = dot(copies[...], matrix, (1, side)).astype(BF16)
        return dot(half, copies_t[...]).astype(BF16) * same[...]

    fwd_load.wait()
    pl.semaphore_wait(barrier, n - 1 + ns - 1)

    def first(k, carry):
        load(fields_h, fields, 0, k).wait()
        for p in range(GROUP // 2):
            c = k * GROUP + 2 * p
            forward_pair(jnp.concatenate([fields[c], fields[c + 1]], -1), fwd, zhi, zlo, p, True)
        put_part(k, forward_depth(depth_f, zhi, zlo))
        to_sibling(0, k).start()

        @pl.when(k > 0)
        def _():
            join(0, k - 1)

        return carry

    lax.fori_loop(0, chunks, first, 0)

    mix[...] = spread(point[...], 1)
    mix_back[...] = spread(point[...], 0)
    column = jnp.sum(copies[...].astype(F32) * bias_row[...], -1, keepdims=True)
    bias[...] = jnp.broadcast_to(column, (flat, PLANE))
    join(0, chunks - 1)

    weight_load.wait()

    def widen(c, carry):
        pair_rows[...] = weight[c].astype(F32)
        w_re[c] = pair_rows[:, 0, :]
        w_im[c] = pair_rows[:, 1, :]
        return carry

    lax.fori_loop(0, channels, widen, 0)

    def pointwise(i, carry):
        at = pl.multiple_of(i * 2 * rows, 2 * rows)
        block = fields[:, pl.ds(at, 2 * rows), :].astype(F32)
        block = jnp.concatenate([block[:, :rows], block[:, rows:]], -1).reshape(flat, 2 * PLANE)
        value = dot(mix[...], block.astype(BF16))
        for k in range(2):
            out = value[:, k * PLANE : (k + 1) * PLANE] + bias[...]
            work[:, pl.ds(pl.multiple_of(at + k * rows, rows), rows), :] = out.reshape(channels, rows, PLANE)
        return carry

    half_lines = NY // 4
    lax.fori_loop(0, half_lines, pointwise, 0, unroll=2)

    def gather_total(e, scale):
        for k in range(chunks):
            for j in range(1, chips):
                to_owner(e, k, j).wait()
            total = joined[e, k, chip]
            for j in range(1, chips):
                total = total + recv[e, k, j - 1]
            total = total * scale
            for g in range(GROUP):
                stage[g] = total[:, g * XY : (g + 1) * XY]
            for j in range(own_rows):
                r, q = j // owned, j % owned
                block = stage[:, j, :]
                lined[r, k * GROUP : (k + 1) * GROUP, q * XY : (q + 1) * XY] = block
                for p in range(per):
                    spec[e, q * per + p, r, k * GROUP : (k + 1) * GROUP] = block[:, p * count : (p + 1) * count]

    def side(e, j):
        goal = lax.rem(mine + j, ns)
        return remote(spec.at[e, goal], got.at[e, j], side_send.at[e, j], side_recv.at[e, j], "sample", goal)

    def scatter_mixed(e):
        for k in range(chunks):
            for j in range(own_rows):
                r, q = j // owned, j % owned
                stage[:, j, :] = mixed[r, k * GROUP : (k + 1) * GROUP, q * XY : (q + 1) * XY]
            modes[e, k, me] = jnp.concatenate([stage[g] for g in range(GROUP)], -1)
            for j in range(chips):
                to_all(e, k, j).start()

    gather_total(0, 1.0)

    def add(c, carry):
        w_r, w_i = w_re[c], w_im[c]
        s_r, s_i = lined[0, pl.ds(c, 1), :], lined[1, pl.ds(c, 1), :]
        return carry[0] + (w_r * s_r - w_i * s_i), carry[1] + (w_r * s_i + w_i * s_r)

    zero = jnp.zeros((channels, owned * XY), F32)
    real, imag = lax.fori_loop(0, channels, add, (zero, zero))
    mixed[0] = real * (1.0 / VOLUME)
    mixed[1] = imag * (1.0 / VOLUME)
    scatter_mixed(0)
    for j in range(1, ns):
        side(0, j).start()
    inv_load.wait()
    lax.fori_loop(half_lines, 2 * half_lines, pointwise, 0, unroll=2)

    def relay(e, k):
        for j in range(1, chips):
            to_all(e, k, j).wait()
            to_relay(e, k, j).start()

    def arrived(e, k):
        to_all(e, k, 0).wait()
        for j in range(1, chips):
            to_relay(e, k, j).wait()

    relay(0, 0)

    def middle(k, carry):
        @pl.when(k + 1 < chunks)
        def _():
            relay(0, k + 1)

        arrived(0, k)
        inverse_depth(modes[0, k].reshape(n * own_rows, GROUP * XY), depth_i, grid)
        load(cot_h, cot, 1, k).wait()
        for p in range(GROUP // 2):
            pre[...] = inverse_pair(inv, grid, p)
            for h in range(2):
                c = k * GROUP + 2 * p + h
                value = pre[:, h * PLANE : (h + 1) * PLANE] + work[c]
                phi = 0.5 * (1.0 + lax.erf(value * (1.0 / math.sqrt(2.0))))
                slope = phi + value * jnp.exp(-0.5 * value * value) * (1.0 / math.sqrt(2.0 * math.pi))
                act[c] = (value * phi).astype(BF16)
                work[c] = cot[c].astype(F32) * slope
            c = k * GROUP + 2 * p
            forward_pair(jnp.concatenate([work[c], work[c + 1]], -1), fwd, zhi, zlo, p, False)

        put_part(k, forward_depth(depth_f, zhi, zlo))
        to_sibling(1, k).start()

        @pl.when(k > 0)
        def _():
            join(1, k - 1)

        return carry

    lax.fori_loop(0, chunks, middle, 0)

    def back(i, carry):
        at = pl.multiple_of(i * 2 * rows, 2 * rows)
        block = work[:, pl.ds(at, 2 * rows), :]
        block = jnp.concatenate([block[:, :rows], block[:, rows:]], -1).reshape(flat, 2 * PLANE)
        high, low = split(block)
        value = dot(mix_back[...], high) + dot(mix_back[...], low)
        for k in range(2):
            out = value[:, k * PLANE : (k + 1) * PLANE].reshape(channels, rows, PLANE)
            local[:, pl.ds(pl.multiple_of(at + k * rows, rows), rows), :] = out
        return carry

    lax.fori_loop(0, half_lines // 2, back, 0, unroll=2)
    join(1, chunks - 1)
    lax.fori_loop(half_lines // 2, 2 * half_lines, back, 0, unroll=2)

    gather_total(1, 1.0 / VOLUME)
    for j in range(1, ns):
        side(1, j).start()

    def reduce(c, carry):
        w_r, w_i = w_re[c], w_im[c]
        u_r, u_i = lined[0], lined[1]
        mixed[0, pl.ds(c, 1), :] = jnp.sum(w_r * u_r + w_i * u_i, 0, keepdims=True)
        mixed[1, pl.ds(c, 1), :] = jnp.sum(w_r * u_i - w_i * u_r, 0, keepdims=True)
        return carry

    lax.fori_loop(0, channels, reduce, 0)
    scatter_mixed(1)
    relay(1, 0)

    for e in range(2):
        for j in range(1, ns):
            side(e, j).wait()
        got[e, 0] = spec[e, mine]

    def term(c, carry):
        real = jnp.zeros((channels, count), F32)
        imag = jnp.zeros((channels, count), F32)
        for s in range(ns):
            a_r, a_i = got[0, s, 0, pl.ds(c, 1), :], got[0, s, 1, pl.ds(c, 1), :]
            b_r, b_i = got[1, s, 0], got[1, s, 1]
            real = real + (a_r * b_r + a_i * b_i)
            imag = imag + (a_r * b_i - a_i * b_r)
        grad[c, :, 0, :] = real
        grad[c, :, 1, :] = imag
        return carry

    lax.fori_loop(0, channels, term, 0)

    def last(k, carry):
        @pl.when(k + 1 < chunks)
        def _():
            relay(1, k + 1)

        arrived(1, k)
        inverse_depth(modes[1, k].reshape(n * own_rows, GROUP * XY), depth_i, grid)
        for p in range(GROUP // 2):
            res = inverse_pair(inv, grid, p)
            for h in range(2):
                c = k * GROUP + 2 * p + h
                out[c] = (res[:, h * PLANE : (h + 1) * PLANE] + local[c]).astype(BF16)
        return carry

    lax.fori_loop(0, chunks, last, 0)


def shards(fields, cotangent, spectral_weight, point_weight, point_bias):
    _, rows, channels, columns = fields.shape
    n = lax.axis_size("space")
    ns = lax.axis_size("sample")
    forward, inverse, depth_f, depth_i = [jnp.asarray(t) for t in tables(rows, n)]
    cells = NY * rows
    chunks = channels // GROUP
    chips = n // 2
    owned = MT * MZ // n
    own_rows = 2 * owned
    width = GROUP * XY
    flat = channels * rows
    count = owned * XY // ns
    copies = np.repeat(np.eye(channels), rows, 0).astype(BF16)
    same = np.tile(np.eye(rows), (channels, channels)).astype(BF16)

    def by_channel(value):
        value = value[0].reshape(rows, channels, NY, PLANE)
        return jnp.transpose(value, (1, 2, 0, 3)).reshape(channels, cells, PLANE)

    def by_row(value):
        value = jnp.transpose(value.reshape(channels, NY, rows, PLANE), (2, 0, 1, 3))
        return value.reshape(1, rows, channels, columns)

    weight = jnp.transpose(spectral_weight, (1, 2, 0, 3))
    vmem, dma = pltpu.VMEM, pltpu.SemaphoreType.DMA
    any_spec, vmem_spec = pl.BlockSpec(memory_space=pltpu.HBM), pl.BlockSpec(memory_space=vmem)
    kept = (ns, 2, channels, count)
    modes_shape = (chunks, n, own_rows, width)

    act, grad_in, grad = pl.pallas_call(
        functools.partial(main_kernel, n, ns),
        out_shape=[
            vmem((channels, cells, PLANE), BF16),
            vmem((channels, cells, PLANE), BF16),
            vmem((channels, channels, 2, count), F32),
        ],
        in_specs=[any_spec] * 5 + [vmem_spec] * 7,
        out_specs=[vmem_spec] * 3,
        scratch_shapes=[
            vmem((channels, cells, PLANE), BF16),
            vmem((channels, cells, PLANE), BF16),
            vmem(weight.shape, BF16),
            vmem(forward.shape[1:], BF16),
            vmem(inverse.shape[1:], BF16),
            vmem((channels, cells, PLANE), F32),
            vmem((channels, cells, PLANE), F32),
            vmem((GROUP, XY, 2 * PLANE), BF16),
            vmem((GROUP, XY, 2 * PLANE), BF16),
            vmem((GROUP, 6 * XY, PLANE), BF16),
            vmem((cells, 2 * PLANE), F32),
            vmem((flat, flat), BF16),
            vmem((flat, flat), BF16),
            vmem((flat, PLANE), F32),
            vmem((channels, 2, owned * XY), F32),
            vmem((channels, channels, owned * XY), F32),
            vmem((channels, channels, owned * XY), F32),
            vmem((chunks, 2, chips * own_rows, width), F32),
            vmem((2, chunks, chips * own_rows, width), F32),
            vmem((2, chunks, chips, own_rows, width), F32),
            vmem((2, chunks, chips - 1, own_rows, width), F32),
            vmem((2,) + modes_shape, F32),
            vmem((GROUP, own_rows, XY), F32),
            vmem((2, channels, owned * XY), F32),
            vmem((2, channels, owned * XY), F32),
            vmem((2,) + kept, F32),
            vmem((2,) + kept, F32),
            dma((2, chunks)), dma((3,)),
            dma((2, chunks)), dma((2, chunks)),
            dma((2, chunks, chips)), dma((2, chunks, chips)),
            dma((2, chunks, chips)), dma((2, chunks, chips)),
            dma((2, chunks, chips)), dma((2, chunks, chips)),
            dma((2, ns)), dma((2, ns)),
        ],
        compiler_params=pltpu.CompilerParams(
            vmem_limit_bytes=VMEM_LIMIT, collective_id=0, has_side_effects=True
        ),
    )(
        by_channel(fields), by_channel(cotangent), weight, forward, inverse, depth_f, depth_i,
        point_weight, point_bias[None], copies, copies.T, same,
    )

    return by_row(act), by_row(grad_in), jnp.transpose(grad, (2, 0, 1, 3))


def solution(mesh):
    return jax.shard_map(
        shards,
        mesh=mesh,
        in_specs=(
            P("sample", "space", None, None),
            P("sample", "space", None, None),
            P(None, None, None, "space"),
            P(),
            P(),
        ),
        out_specs=(
            P("sample", "space", None, None),
            P("sample", "space", None, None),
            P(None, None, None, ("space", "sample")),
        ),
        check_vma=False,
    )
```

```python
import functools
import math

import jax
import jax.numpy as jnp
import numpy as np
from jax import lax
from jax.experimental import pallas as pl
from jax.experimental.pallas import tpu as pltpu
from jax.sharding import PartitionSpec as P

NX, NY, NZ, NT = 64, 64, 32, 4
MX, MY, MZ, MT = 12, 12, 8, 4
VOLUME = NX * NY * NZ * NT
PLANE = NZ * NT
XY = MX * MY
BF16, F32 = jnp.bfloat16, jnp.float32
VMEM_LIMIT = 60_970_000
GROUP = 4
MESH = pl.DeviceIdType.MESH


def signed(modes):
    index = np.arange(modes)
    return np.where(index < modes // 2, index, index - modes)


def split_np(table):
    high = table.astype(np.float32).astype(BF16)
    low = (table - high.astype(np.float64)).astype(np.float32).astype(BF16)
    return high, low


def tables(rows, space):
    fy, fx = signed(MY), signed(MX)
    y = np.arange(NY)
    x = np.arange(space * rows).reshape(space, rows)
    phi = 2 * np.pi * (
        (fy.reshape(1, MY, 1, 1, 1) * y.reshape(1, 1, 1, NY, 1) % NY) / NY
        + (fx.reshape(1, 1, MX, 1, 1) * x.reshape(space, 1, 1, 1, rows) % NX) / NX
    ).reshape(space, XY, NY * rows)
    plane = np.concatenate([np.cos(phi), np.sin(phi)], 1)
    hi, lo = split_np(plane)
    forward = np.concatenate([hi, lo], 1)
    turned = lambda t: np.transpose(t, (0, 2, 1))
    inverse = np.concatenate([turned(hi), turned(lo), turned(hi)], 2)
    fz, ft = signed(MZ), signed(MT)
    z, t = np.arange(NZ), np.arange(NT)
    psi = 2 * np.pi * (
        fz.reshape(MZ, 1, 1, 1) * z.reshape(1, 1, NZ, 1) / NZ
        + ft.reshape(1, MT, 1, 1) * t.reshape(1, 1, 1, NT) / NT
    ).reshape(space, MZ * MT // space, PLANE)
    cos, sin = np.cos(psi), np.sin(psi)
    depth = np.stack(
        [np.concatenate([cos, -sin], -1), np.concatenate([-sin, -cos], -1)], 1
    ).reshape(space, 2 * MZ * MT // space, 2 * PLANE)
    dhi, dlo = split_np(depth)
    flat = lambda t: t.reshape(2 * MZ * MT, 2 * PLANE)
    by_core = lambda t: flat(np.concatenate([t[0::2], t[1::2]], 0))
    depth_forward = np.concatenate([by_core(dhi), by_core(dlo)], 0)
    depth_inverse = np.concatenate([flat(dhi), flat(dhi), flat(dlo)], 0)
    return forward, inverse, depth_forward, depth_inverse


def split(value):
    high = value.astype(BF16)
    return high, (value - high.astype(F32)).astype(BF16)


def dot(a, b, contract=(1, 0)):
    dims = (((contract[0],), (contract[1],)), ((), ()))
    return lax.dot_general(a, b, dims, preferred_element_type=F32)


def forward_pair(block, fwd, zhi, zlo, p, exact):
    half = fwd.shape[0] // 2
    if exact:
        res = dot(fwd[...], block)
        res = res[:half] + res[half:]
    else:
        high, low = split(block)
        res = dot(fwd[...], high)
        res = res[:half] + res[half:] + dot(fwd[:half], low)
    for k in range(2):
        part = res[:, k * PLANE : (k + 1) * PLANE]
        high, low = split(jnp.concatenate([part[:XY], part[XY:]], -1))
        zhi[2 * p + k] = high
        zlo[2 * p + k] = low


def forward_depth(depth, zhi, zlo):
    rows = depth.shape[0] // 2
    high = zhi[...].reshape(-1, 2 * PLANE)
    low = zlo[...].reshape(-1, 2 * PLANE)
    first = dot(depth[...], high, (1, 1))
    return first[:rows] + first[rows:] + dot(depth[:rows], low, (1, 1))


def inverse_depth(modes, depth, grid):
    high, low = split(modes)
    stacked = jnp.concatenate([high, low, high], 0)
    lines = dot(stacked, depth[...], (0, 0)).reshape(GROUP, XY, 2 * PLANE)
    high, low = split(lines)
    for at, value in ((0, high), (2 * XY, high), (4 * XY, low)):
        grid[:, at : at + XY] = value[:, :, :PLANE]
        grid[:, at + XY : at + 2 * XY] = value[:, :, PLANE:]


def inverse_pair(inv, grid, p):
    return dot(inv[...], jnp.concatenate([grid[2 * p], grid[2 * p + 1]], -1))


def main_kernel(
    n, ns,
    fields_h, cot_h, weight_h, fwd_h, inv_h, *refs,
):
    smalls_h, (act, out, grad), smalls, refs = refs[:7], refs[7:10], refs[10:17], refs[17:]
    depth_f, depth_i, point, bias_row, copies, copies_t, same = smalls
    (fields, cot, weight, fwd, inv, work, local, zhi, zlo, grid, pre, mix, mix_back, bias, pair_rows, w_re, w_im,
     part, near, joined, recv, modes, stage, lined, mixed, spec, got,
     load_sem, table_sem, small_sem,
     near_send, near_recv, sum_send, sum_recv, all_send, all_recv, relay_send, relay_recv, side_send, side_recv) = refs
    channels, cells, _ = fields.shape
    chunks = channels // GROUP
    rows = cells // NY
    flat = channels * rows
    chips = n // 2
    own_rows = stage.shape[1]
    owned = own_rows // 2
    per = ns // owned
    count = owned * XY // ns
    me = lax.axis_index("space")
    mine = lax.axis_index("sample")
    core = lax.rem(me, 2)
    chip = (me - core) // 2
    sibling = me + 1 - 2 * core

    barrier = pltpu.get_barrier_semaphore()
    for k in range(1, n):
        pl.semaphore_signal(barrier, inc=1, device_id={"space": lax.rem(me + k, n)}, device_id_type=MESH)
    for k in range(1, ns):
        pl.semaphore_signal(barrier, inc=1, device_id={"sample": lax.rem(mine + k, ns)}, device_id_type=MESH)

    def group(k):
        return pl.ds(k * GROUP, GROUP)

    def load(src, dst, which, k):
        return pltpu.make_async_copy(src.at[group(k)], dst.at[group(k)], load_sem.at[which, k])

    fwd_load = pltpu.make_async_copy(fwd_h.at[me], fwd, table_sem.at[0])
    inv_load = pltpu.make_async_copy(inv_h.at[me], inv, table_sem.at[1])
    weight_load = pltpu.make_async_copy(weight_h, weight, table_sem.at[2])
    small_loads = [
        pltpu.make_async_copy(src, dst, small_sem.at[i]) for i, (src, dst) in enumerate(zip(smalls_h, smalls))
    ]
    fwd_load.start()
    load(fields_h, fields, 0, 0).start()
    for copy in small_loads:
        copy.start()
    for k in range(1, chunks):
        load(fields_h, fields, 0, k).start()
    weight_load.start()
    inv_load.start()
    for k in range(chunks):
        load(cot_h, cot, 1, k).start()

    def remote(src, dst, send, got_sem, axis, target):
        return pltpu.make_async_remote_copy(
            src_ref=src, dst_ref=dst, send_sem=send, recv_sem=got_sem,
            device_id={axis: target}, device_id_type=MESH,
        )

    def to_sibling(e, k):
        return remote(part.at[k, 1 - core], near.at[e, k], near_send.at[e, k], near_recv.at[e, k], "space", sibling)

    def to_owner(e, k, j):
        goal = lax.rem(chip + j, chips)
        return remote(
            joined.at[e, k, goal], recv.at[e, k, j - 1], sum_send.at[e, k, j], sum_recv.at[e, k, j], "space", 2 * goal + core
        )

    def to_all(e, k, j):
        target = lax.rem(me + 2 * j, n) if j else sibling
        return remote(modes.at[e, k, me], modes.at[e, k, me], all_send.at[e, k, j], all_recv.at[e, k, j], "space", target)

    def to_relay(e, k, j):
        block = modes.at[e, k, lax.rem(me + n - 2 * j, n)]
        return remote(block, block, relay_send.at[e, k, j], relay_recv.at[e, k, j], "space", sibling)

    def join(e, k):
        to_sibling(e, k).wait()
        total = part[k, core] + near[e, k]
        for j in range(chips):
            joined[e, k, j] = total[j * own_rows : (j + 1) * own_rows]
        for j in range(1, chips):
            to_owner(e, k, j).start()

    def put_part(k, value):
        half = value.shape[0] // 2
        part[k, 0] = value[:half]
        part[k, 1] = value[half:]

    def spread(matrix, side):
        half = dot(copies[...], matrix, (1, side)).astype(BF16)
        return dot(half, copies_t[...]).astype(BF16) * same[...]

    fwd_load.wait()

    def transform(k):
        load(fields_h, fields, 0, k).wait()
        for p in range(GROUP // 2):
            c = k * GROUP + 2 * p
            forward_pair(jnp.concatenate([fields[c], fields[c + 1]], -1), fwd, zhi, zlo, p, True)

    def first(k, carry):
        transform(k)
        put_part(k, forward_depth(depth_f, zhi, zlo))
        to_sibling(0, k).start()
        join(0, k - 1)
        return carry

    transform(0)
    for copy in small_loads:
        copy.wait()
    put_part(0, forward_depth(depth_f, zhi, zlo))
    pl.semaphore_wait(barrier, n - 1 + ns - 1)
    to_sibling(0, 0).start()
    lax.fori_loop(1, chunks, first, 0)

    mix[...] = spread(point[...], 1)
    mix_back[...] = spread(point[...], 0)
    column = jnp.sum(copies[...].astype(F32) * bias_row[...], -1, keepdims=True)
    bias[...] = jnp.broadcast_to(column, (flat, PLANE))
    join(0, chunks - 1)

    weight_load.wait()

    def widen(c, carry):
        pair_rows[...] = weight[c].astype(F32)
        w_re[c] = pair_rows[:, 0, :]
        w_im[c] = pair_rows[:, 1, :]
        return carry

    lax.fori_loop(0, channels, widen, 0)

    def pointwise(i, carry):
        at = pl.multiple_of(i * 2 * rows, 2 * rows)
        block = fields[:, pl.ds(at, 2 * rows), :].astype(F32)
        block = jnp.concatenate([block[:, :rows], block[:, rows:]], -1).reshape(flat, 2 * PLANE)
        value = dot(mix[...], block.astype(BF16))
        for k in range(2):
            out = value[:, k * PLANE : (k + 1) * PLANE] + bias[...]
            work[:, pl.ds(pl.multiple_of(at + k * rows, rows), rows), :] = out.reshape(channels, rows, PLANE)
        return carry

    half_lines = NY // 4
    lax.fori_loop(0, half_lines, pointwise, 0, unroll=2)

    def gather_total(e, scale, use=None):
        for k in range(chunks):
            for j in range(1, chips):
                to_owner(e, k, j).wait()
            total = joined[e, k, chip]
            for j in range(1, chips):
                total = total + recv[e, k, j - 1]
            total = total * scale
            for g in range(GROUP):
                stage[g] = total[:, g * XY : (g + 1) * XY]
            for j in range(own_rows):
                r, q = j // owned, j % owned
                block = stage[:, j, :]
                lined[r, k * GROUP : (k + 1) * GROUP, q * XY : (q + 1) * XY] = block
                for p in range(per):
                    spec[e, q * per + p, r, k * GROUP : (k + 1) * GROUP] = block[:, p * count : (p + 1) * count]
            if use is not None:
                use(k)

    def side(e, j):
        goal = lax.rem(mine + j, ns)
        return remote(spec.at[e, goal], got.at[e, j], side_send.at[e, j], side_recv.at[e, j], "sample", goal)

    def scatter_mixed(e):
        for k in range(chunks):
            for j in range(own_rows):
                r, q = j // owned, j % owned
                stage[:, j, :] = mixed[r, k * GROUP : (k + 1) * GROUP, q * XY : (q + 1) * XY]
            modes[e, k, me] = jnp.concatenate([stage[g] for g in range(GROUP)], -1)
            for j in range(chips):
                to_all(e, k, j).start()

    def add(k):
        real, imag = (mixed[0], mixed[1]) if k else (0.0, 0.0)
        for c in range(k * GROUP, (k + 1) * GROUP):
            w_r, w_i = w_re[c], w_im[c]
            s_r, s_i = lined[0, c : c + 1, :], lined[1, c : c + 1, :]
            real = real + (w_r * s_r - w_i * s_i)
            imag = imag + (w_r * s_i + w_i * s_r)
        scale = 1.0 / VOLUME if k == chunks - 1 else 1.0
        mixed[0] = real * scale
        mixed[1] = imag * scale

    gather_total(0, 1.0, add)
    scatter_mixed(0)
    for j in range(1, ns):
        side(0, j).start()
    inv_load.wait()
    lax.fori_loop(half_lines, 2 * half_lines, pointwise, 0, unroll=2)

    def relay(e, k):
        for j in range(1, chips):
            to_all(e, k, j).wait()
            to_relay(e, k, j).start()

    def arrived(e, k):
        to_all(e, k, 0).wait()
        for j in range(1, chips):
            to_relay(e, k, j).wait()

    relay(0, 0)

    def middle(k, carry):
        @pl.when(k + 1 < chunks)
        def _():
            relay(0, k + 1)

        arrived(0, k)
        inverse_depth(modes[0, k].reshape(n * own_rows, GROUP * XY), depth_i, grid)
        load(cot_h, cot, 1, k).wait()
        for p in range(GROUP // 2):
            pre[...] = inverse_pair(inv, grid, p)
            for h in range(2):
                c = k * GROUP + 2 * p + h
                value = pre[:, h * PLANE : (h + 1) * PLANE] + work[c]
                phi = 0.5 * (1.0 + lax.erf(value * (1.0 / math.sqrt(2.0))))
                slope = phi + value * jnp.exp(-0.5 * value * value) * (1.0 / math.sqrt(2.0 * math.pi))
                act[c] = (value * phi).astype(BF16)
                work[c] = cot[c].astype(F32) * slope
            c = k * GROUP + 2 * p
            forward_pair(jnp.concatenate([work[c], work[c + 1]], -1), fwd, zhi, zlo, p, False)

        put_part(k, forward_depth(depth_f, zhi, zlo))
        to_sibling(1, k).start()

        @pl.when(k > 0)
        def _():
            join(1, k - 1)

        return carry

    lax.fori_loop(0, chunks, middle, 0)

    def back(i, carry):
        at = pl.multiple_of(i * 2 * rows, 2 * rows)
        block = work[:, pl.ds(at, 2 * rows), :]
        block = jnp.concatenate([block[:, :rows], block[:, rows:]], -1).reshape(flat, 2 * PLANE)
        high, low = split(block)
        value = dot(mix_back[...], high) + dot(mix_back[...], low)
        for k in range(2):
            out = value[:, k * PLANE : (k + 1) * PLANE].reshape(channels, rows, PLANE)
            local[:, pl.ds(pl.multiple_of(at + k * rows, rows), rows), :] = out
        return carry

    lax.fori_loop(0, half_lines // 2, back, 0, unroll=2)
    join(1, chunks - 1)
    lax.fori_loop(half_lines // 2, 2 * half_lines, back, 0, unroll=2)

    gather_total(1, 1.0 / VOLUME)
    for j in range(1, ns):
        side(1, j).start()

    def reduce(c, carry):
        w_r, w_i = w_re[c], w_im[c]
        u_r, u_i = lined[0], lined[1]
        mixed[0, pl.ds(c, 1), :] = jnp.sum(w_r * u_r + w_i * u_i, 0, keepdims=True)
        mixed[1, pl.ds(c, 1), :] = jnp.sum(w_r * u_i - w_i * u_r, 0, keepdims=True)
        return carry

    lax.fori_loop(0, channels, reduce, 0)
    scatter_mixed(1)
    relay(1, 0)

    for e in range(2):
        for j in range(1, ns):
            side(e, j).wait()
        got[e, 0] = spec[e, mine]

    def term(c, carry):
        real = jnp.zeros((channels, count), F32)
        imag = jnp.zeros((channels, count), F32)
        for s in range(ns):
            a_r, a_i = got[0, s, 0, pl.ds(c, 1), :], got[0, s, 1, pl.ds(c, 1), :]
            b_r, b_i = got[1, s, 0], got[1, s, 1]
            real = real + (a_r * b_r + a_i * b_i)
            imag = imag + (a_r * b_i - a_i * b_r)
        grad[c, :, 0, :] = real
        grad[c, :, 1, :] = imag
        return carry

    lax.fori_loop(0, channels, term, 0)

    def last(k, carry):
        @pl.when(k + 1 < chunks)
        def _():
            relay(1, k + 1)

        arrived(1, k)
        inverse_depth(modes[1, k].reshape(n * own_rows, GROUP * XY), depth_i, grid)
        for p in range(GROUP // 2):
            res = inverse_pair(inv, grid, p)
            for h in range(2):
                c = k * GROUP + 2 * p + h
                out[c] = (res[:, h * PLANE : (h + 1) * PLANE] + local[c]).astype(BF16)
        return carry

    lax.fori_loop(0, chunks, last, 0)


def store_kernel(*refs):
    sources, goals, sem = refs[:3], refs[3:6], refs[6]
    copies = [pltpu.make_async_copy(a, b, sem.at[i]) for i, (a, b) in enumerate(zip(sources, goals))]
    for copy in copies:
        copy.start()
    for copy in copies:
        copy.wait()


def shards(fields, cotangent, spectral_weight, point_weight, point_bias):
    _, rows, channels, columns = fields.shape
    n = lax.axis_size("space")
    ns = lax.axis_size("sample")
    forward, inverse, depth_f, depth_i = [jnp.asarray(t) for t in tables(rows, n)]
    cells = NY * rows
    chunks = channels // GROUP
    chips = n // 2
    owned = MT * MZ // n
    own_rows = 2 * owned
    width = GROUP * XY
    flat = channels * rows
    count = owned * XY // ns
    copies = np.repeat(np.eye(channels), rows, 0).astype(BF16)
    same = np.tile(np.eye(rows), (channels, channels)).astype(BF16)

    def by_channel(value):
        value = value[0].reshape(rows, channels, NY, PLANE)
        return jnp.transpose(value, (1, 2, 0, 3)).reshape(channels, cells, PLANE)

    def by_row(value):
        value = jnp.transpose(value.reshape(channels, NY, rows, PLANE), (2, 0, 1, 3))
        return value.reshape(1, rows, channels, columns)

    weight = jnp.transpose(spectral_weight, (1, 2, 0, 3))
    vmem, dma = pltpu.VMEM, pltpu.SemaphoreType.DMA
    any_spec, vmem_spec = pl.BlockSpec(memory_space=pltpu.HBM), pl.BlockSpec(memory_space=vmem)
    kept = (ns, 2, channels, count)
    modes_shape = (chunks, n, own_rows, width)

    smalls = [depth_f, depth_i, point_weight, point_bias[None], copies, copies.T, same]
    act, grad_in, grad = pl.pallas_call(
        functools.partial(main_kernel, n, ns),
        out_shape=[
            vmem((channels, cells, PLANE), BF16),
            vmem((channels, cells, PLANE), BF16),
            vmem((channels, channels, 2, count), F32),
        ],
        in_specs=[any_spec] * 12,
        out_specs=[vmem_spec] * 3,
        scratch_shapes=[vmem(t.shape, t.dtype) for t in smalls] + [
            vmem((channels, cells, PLANE), BF16),
            vmem((channels, cells, PLANE), BF16),
            vmem(weight.shape, BF16),
            vmem(forward.shape[1:], BF16),
            vmem(inverse.shape[1:], BF16),
            vmem((channels, cells, PLANE), F32),
            vmem((channels, cells, PLANE), F32),
            vmem((GROUP, XY, 2 * PLANE), BF16),
            vmem((GROUP, XY, 2 * PLANE), BF16),
            vmem((GROUP, 6 * XY, PLANE), BF16),
            vmem((cells, 2 * PLANE), F32),
            vmem((flat, flat), BF16),
            vmem((flat, flat), BF16),
            vmem((flat, PLANE), F32),
            vmem((channels, 2, owned * XY), F32),
            vmem((channels, channels, owned * XY), F32),
            vmem((channels, channels, owned * XY), F32),
            vmem((chunks, 2, chips * own_rows, width), F32),
            vmem((2, chunks, chips * own_rows, width), F32),
            vmem((2, chunks, chips, own_rows, width), F32),
            vmem((2, chunks, chips - 1, own_rows, width), F32),
            vmem((2,) + modes_shape, F32),
            vmem((GROUP, own_rows, XY), F32),
            vmem((2, channels, owned * XY), F32),
            vmem((2, channels, owned * XY), F32),
            vmem((2,) + kept, F32),
            vmem((2,) + kept, F32),
            dma((2, chunks)), dma((3,)), dma((7,)),
            dma((2, chunks)), dma((2, chunks)),
            dma((2, chunks, chips)), dma((2, chunks, chips)),
            dma((2, chunks, chips)), dma((2, chunks, chips)),
            dma((2, chunks, chips)), dma((2, chunks, chips)),
            dma((2, ns)), dma((2, ns)),
        ],
        compiler_params=pltpu.CompilerParams(
            vmem_limit_bytes=VMEM_LIMIT, collective_id=0, has_side_effects=True
        ),
    )(
        by_channel(fields), by_channel(cotangent), weight, forward, inverse, *smalls
    )

    act, grad_in, grad = pl.pallas_call(
        store_kernel,
        out_shape=[jax.ShapeDtypeStruct(v.shape, v.dtype) for v in (act, grad_in, grad)],
        in_specs=[vmem_spec] * 3,
        out_specs=[any_spec] * 3,
        scratch_shapes=[dma((3,))],
        compiler_params=pltpu.CompilerParams(vmem_limit_bytes=512 * 1024),
    )(act, grad_in, grad)
    return by_row(act), by_row(grad_in), jnp.transpose(grad, (2, 0, 1, 3))


def solution(mesh):
    return jax.shard_map(
        shards,
        mesh=mesh,
        in_specs=(
            P("sample", "space", None, None),
            P("sample", "space", None, None),
            P(None, None, None, "space"),
            P(),
            P(),
        ),
        out_specs=(
            P("sample", "space", None, None),
            P("sample", "space", None, None),
            P(None, None, None, ("space", "sample")),
        ),
        check_vma=False,
    )
```

```python
import functools
import math

import jax
import jax.numpy as jnp
import numpy as np
from jax import lax
from jax.experimental import pallas as pl
from jax.experimental.pallas import tpu as pltpu
from jax.sharding import PartitionSpec as P

NX, NY, NZ, NT = 64, 64, 32, 4
MX, MY, MZ, MT = 12, 12, 8, 4
VOLUME = NX * NY * NZ * NT
PLANE = NZ * NT
XY = MX * MY
BF16, F32 = jnp.bfloat16, jnp.float32
VMEM_LIMIT = 60_970_000
GROUP = 4
MESH = pl.DeviceIdType.MESH


def signed(modes):
    index = np.arange(modes)
    return np.where(index < modes // 2, index, index - modes)


def split_np(table):
    high = table.astype(np.float32).astype(BF16)
    low = (table - high.astype(np.float64)).astype(np.float32).astype(BF16)
    return high, low


def tables(rows, space):
    fy, fx = signed(MY), signed(MX)
    y = np.arange(NY)
    x = np.arange(space * rows).reshape(space, rows)
    phi = 2 * np.pi * (
        (fy.reshape(1, MY, 1, 1, 1) * y.reshape(1, 1, 1, NY, 1) % NY) / NY
        + (fx.reshape(1, 1, MX, 1, 1) * x.reshape(space, 1, 1, 1, rows) % NX) / NX
    ).reshape(space, XY, NY * rows)
    plane = np.concatenate([np.cos(phi), np.sin(phi)], 1)
    hi, lo = split_np(plane)
    forward = np.concatenate([hi, lo], 1)
    turned = lambda t: np.transpose(t, (0, 2, 1))
    inverse = np.concatenate([turned(hi), turned(lo), turned(hi)], 2)
    fz, ft = signed(MZ), signed(MT)
    z, t = np.arange(NZ), np.arange(NT)
    psi = 2 * np.pi * (
        fz.reshape(MZ, 1, 1, 1) * z.reshape(1, 1, NZ, 1) / NZ
        + ft.reshape(1, MT, 1, 1) * t.reshape(1, 1, 1, NT) / NT
    ).reshape(space, MZ * MT // space, PLANE)
    cos, sin = np.cos(psi), np.sin(psi)
    depth = np.stack(
        [np.concatenate([cos, -sin], -1), np.concatenate([-sin, -cos], -1)], 1
    ).reshape(space, 2 * MZ * MT // space, 2 * PLANE)
    dhi, dlo = split_np(depth)
    flat = lambda t: t.reshape(2 * MZ * MT, 2 * PLANE)
    by_core = lambda t: flat(np.concatenate([t[0::2], t[1::2]], 0))
    depth_forward = np.concatenate([by_core(dhi), by_core(dlo)], 0)
    depth_inverse = np.concatenate([flat(dhi), flat(dhi), flat(dlo)], 0)
    return forward, inverse, depth_forward, depth_inverse


def split(value):
    high = value.astype(BF16)
    return high, (value - high.astype(F32)).astype(BF16)


def dot(a, b, contract=(1, 0)):
    dims = (((contract[0],), (contract[1],)), ((), ()))
    return lax.dot_general(a, b, dims, preferred_element_type=F32)


def forward_pair(block, fwd, zhi, zlo, p, exact):
    half = fwd.shape[0] // 2
    if exact:
        res = dot(fwd[...], block)
        res = res[:half] + res[half:]
    else:
        high, low = split(block)
        res = dot(fwd[...], high)
        res = res[:half] + res[half:] + dot(fwd[:half], low)
    for k in range(2):
        part = res[:, k * PLANE : (k + 1) * PLANE]
        high, low = split(jnp.concatenate([part[:XY], part[XY:]], -1))
        zhi[2 * p + k] = high
        zlo[2 * p + k] = low


def forward_depth(depth, zhi, zlo):
    rows = depth.shape[0] // 2
    high = zhi[...].reshape(-1, 2 * PLANE)
    low = zlo[...].reshape(-1, 2 * PLANE)
    first = dot(depth[...], high, (1, 1))
    return first[:rows] + first[rows:] + dot(depth[:rows], low, (1, 1))


def inverse_depth(modes, depth, grid):
    high, low = split(modes)
    stacked = jnp.concatenate([high, low, high], 0)
    lines = dot(stacked, depth[...], (0, 0)).reshape(GROUP, XY, 2 * PLANE)
    high, low = split(lines)
    for at, value in ((0, high), (2 * XY, high), (4 * XY, low)):
        grid[:, at : at + XY] = value[:, :, :PLANE]
        grid[:, at + XY : at + 2 * XY] = value[:, :, PLANE:]


def inverse_pair(inv, grid, p):
    return dot(inv[...], jnp.concatenate([grid[2 * p], grid[2 * p + 1]], -1))


def main_kernel(
    n, ns,
    fields_h, cot_h, weight_h, fwd_h, inv_h, *refs,
):
    smalls_h, (act, out, grad), smalls, refs = refs[:7], refs[7:10], refs[10:17], refs[17:]
    depth_f, depth_i, point, bias_row, copies, copies_t, same = smalls
    (fields, cot, weight, fwd, inv, work, local, zhi, zlo, grid, pre, mix, mix_back, bias, pair_rows, w_re, w_im,
     part, near, joined, recv, modes, stage, lined, mixed, spec, got,
     load_sem, table_sem, small_sem,
     near_send, near_recv, sum_send, sum_recv, all_send, all_recv, relay_send, relay_recv, side_send, side_recv) = refs
    channels, cells, _ = fields.shape
    chunks = channels // GROUP
    rows = cells // NY
    flat = channels * rows
    chips = n // 2
    own_rows = stage.shape[1]
    owned = own_rows // 2
    per = ns // owned
    count = owned * XY // ns
    me = lax.axis_index("space")
    mine = lax.axis_index("sample")
    core = lax.rem(me, 2)
    chip = (me - core) // 2
    sibling = me + 1 - 2 * core

    barrier = pltpu.get_barrier_semaphore()
    for k in range(1, n):
        pl.semaphore_signal(barrier, inc=1, device_id={"space": lax.rem(me + k, n)}, device_id_type=MESH)
    for k in range(1, ns):
        pl.semaphore_signal(barrier, inc=1, device_id={"sample": lax.rem(mine + k, ns)}, device_id_type=MESH)

    def group(k):
        return pl.ds(k * GROUP, GROUP)

    def load(src, dst, which, k):
        return pltpu.make_async_copy(src.at[group(k)], dst.at[group(k)], load_sem.at[which, k])

    fwd_load = pltpu.make_async_copy(fwd_h.at[me], fwd, table_sem.at[0])
    inv_load = pltpu.make_async_copy(inv_h.at[me], inv, table_sem.at[1])
    weight_load = pltpu.make_async_copy(weight_h, weight, table_sem.at[2])
    small_loads = [
        pltpu.make_async_copy(src, dst, small_sem.at[i]) for i, (src, dst) in enumerate(zip(smalls_h, smalls))
    ]
    fwd_load.start()
    load(fields_h, fields, 0, 0).start()
    for copy in small_loads:
        copy.start()
    for k in range(1, chunks):
        load(fields_h, fields, 0, k).start()
    weight_load.start()
    inv_load.start()
    for k in range(chunks):
        load(cot_h, cot, 1, k).start()

    def remote(src, dst, send, got_sem, axis, target):
        return pltpu.make_async_remote_copy(
            src_ref=src, dst_ref=dst, send_sem=send, recv_sem=got_sem,
            device_id={axis: target}, device_id_type=MESH,
        )

    def to_sibling(e, k):
        return remote(part.at[k, 1 - core], near.at[e, k], near_send.at[e, k], near_recv.at[e, k], "space", sibling)

    def partner(j):
        if chips == 4:
            pair = (chip, 3 - chip, lax.rem(chip + 2, 4), chip + 1 - 2 * lax.rem(chip, 2))[j]
            return pair, pair
        return lax.rem(chip + j, chips), lax.rem(chip + chips - j, chips)

    def to_owner(e, k, j):
        goal = partner(j)[0]
        return remote(
            joined.at[e, k, goal], recv.at[e, k, j - 1], sum_send.at[e, k, j], sum_recv.at[e, k, j], "space", 2 * goal + core
        )

    def to_all(e, k, j):
        target = 2 * partner(j)[0] + core if j else sibling
        return remote(modes.at[e, k, me], modes.at[e, k, me], all_send.at[e, k, j], all_recv.at[e, k, j], "space", target)

    def to_relay(e, k, j):
        block = modes.at[e, k, 2 * partner(j)[1] + core]
        return remote(block, block, relay_send.at[e, k, j], relay_recv.at[e, k, j], "space", sibling)

    def join(e, k):
        to_sibling(e, k).wait()
        total = part[k, core] + near[e, k]
        for j in range(chips):
            joined[e, k, j] = total[j * own_rows : (j + 1) * own_rows]
        for j in range(1, chips):
            to_owner(e, k, j).start()

    def put_part(k, value):
        half = value.shape[0] // 2
        part[k, 0] = value[:half]
        part[k, 1] = value[half:]

    def spread(matrix, side):
        half = dot(copies[...], matrix, (1, side)).astype(BF16)
        return dot(half, copies_t[...]).astype(BF16) * same[...]

    fwd_load.wait()

    def transform(k):
        load(fields_h, fields, 0, k).wait()
        for p in range(GROUP // 2):
            c = k * GROUP + 2 * p
            forward_pair(jnp.concatenate([fields[c], fields[c + 1]], -1), fwd, zhi, zlo, p, True)

    def first(k, carry):
        transform(k)
        put_part(k, forward_depth(depth_f, zhi, zlo))
        to_sibling(0, k).start()
        join(0, k - 1)
        return carry

    transform(0)
    for copy in small_loads:
        copy.wait()
    put_part(0, forward_depth(depth_f, zhi, zlo))
    pl.semaphore_wait(barrier, n - 1 + ns - 1)
    to_sibling(0, 0).start()
    lax.fori_loop(1, chunks, first, 0)

    mix[...] = spread(point[...], 1)
    mix_back[...] = spread(point[...], 0)
    column = jnp.sum(copies[...].astype(F32) * bias_row[...], -1, keepdims=True)
    bias[...] = jnp.broadcast_to(column, (flat, PLANE))
    join(0, chunks - 1)

    weight_load.wait()

    def widen(c, carry):
        pair_rows[...] = weight[c].astype(F32)
        w_re[c] = pair_rows[:, 0, :]
        w_im[c] = pair_rows[:, 1, :]
        return carry

    lax.fori_loop(0, channels, widen, 0)

    def pointwise(i, carry):
        at = pl.multiple_of(i * 2 * rows, 2 * rows)
        block = fields[:, pl.ds(at, 2 * rows), :].astype(F32)
        block = jnp.concatenate([block[:, :rows], block[:, rows:]], -1).reshape(flat, 2 * PLANE)
        value = dot(mix[...], block.astype(BF16))
        for k in range(2):
            out = value[:, k * PLANE : (k + 1) * PLANE] + bias[...]
            work[:, pl.ds(pl.multiple_of(at + k * rows, rows), rows), :] = out.reshape(channels, rows, PLANE)
        return carry

    half_lines = NY // 4
    lax.fori_loop(0, half_lines, pointwise, 0, unroll=2)

    def gather_total(e, scale, use=None):
        for k in range(chunks):
            for j in range(1, chips):
                to_owner(e, k, j).wait()
            total = joined[e, k, chip]
            for j in range(1, chips):
                total = total + recv[e, k, j - 1]
            total = total * scale
            for g in range(GROUP):
                stage[g] = total[:, g * XY : (g + 1) * XY]
            for j in range(own_rows):
                r, q = j // owned, j % owned
                block = stage[:, j, :]
                lined[r, k * GROUP : (k + 1) * GROUP, q * XY : (q + 1) * XY] = block
                for p in range(per):
                    spec[e, q * per + p, r, k * GROUP : (k + 1) * GROUP] = block[:, p * count : (p + 1) * count]
            if use is not None:
                use(k)

    def side(e, j):
        goal = lax.rem(mine + j, ns)
        return remote(spec.at[e, goal], got.at[e, j], side_send.at[e, j], side_recv.at[e, j], "sample", goal)

    def scatter_mixed(e):
        for k in range(chunks):
            for j in range(own_rows):
                r, q = j // owned, j % owned
                stage[:, j, :] = mixed[r, k * GROUP : (k + 1) * GROUP, q * XY : (q + 1) * XY]
            modes[e, k, me] = jnp.concatenate([stage[g] for g in range(GROUP)], -1)
            for j in list(range(1, chips)) + [0]:
                to_all(e, k, j).start()

    def add(k):
        real, imag = (mixed[0], mixed[1]) if k else (0.0, 0.0)
        for c in range(k * GROUP, (k + 1) * GROUP):
            w_r, w_i = w_re[c], w_im[c]
            s_r, s_i = lined[0, c : c + 1, :], lined[1, c : c + 1, :]
            real = real + (w_r * s_r - w_i * s_i)
            imag = imag + (w_r * s_i + w_i * s_r)
        scale = 1.0 / VOLUME if k == chunks - 1 else 1.0
        mixed[0] = real * scale
        mixed[1] = imag * scale

    gather_total(0, 1.0, add)
    scatter_mixed(0)
    for j in range(1, ns):
        side(0, j).start()
    inv_load.wait()
    lax.fori_loop(half_lines, 2 * half_lines, pointwise, 0, unroll=2)

    def relay(e, k):
        for j in range(1, chips):
            to_all(e, k, j).wait()
            to_relay(e, k, j).start()

    def arrived(e, k):
        to_all(e, k, 0).wait()
        for j in range(1, chips):
            to_relay(e, k, j).wait()

    relay(0, 0)

    def middle(k, carry):
        @pl.when(k + 1 < chunks)
        def _():
            relay(0, k + 1)

        arrived(0, k)
        inverse_depth(modes[0, k].reshape(n * own_rows, GROUP * XY), depth_i, grid)
        load(cot_h, cot, 1, k).wait()
        for p in range(GROUP // 2):
            pre[...] = inverse_pair(inv, grid, p)
            for h in range(2):
                c = k * GROUP + 2 * p + h
                value = pre[:, h * PLANE : (h + 1) * PLANE] + work[c]
                phi = 0.5 * (1.0 + lax.erf(value * (1.0 / math.sqrt(2.0))))
                slope = phi + value * jnp.exp(-0.5 * value * value) * (1.0 / math.sqrt(2.0 * math.pi))
                act[c] = (value * phi).astype(BF16)
                work[c] = cot[c].astype(F32) * slope
            c = k * GROUP + 2 * p
            forward_pair(jnp.concatenate([work[c], work[c + 1]], -1), fwd, zhi, zlo, p, False)

        put_part(k, forward_depth(depth_f, zhi, zlo))
        to_sibling(1, k).start()

        @pl.when(k > 0)
        def _():
            join(1, k - 1)

        return carry

    lax.fori_loop(0, chunks, middle, 0)

    def back(i, carry):
        at = pl.multiple_of(i * 2 * rows, 2 * rows)
        block = work[:, pl.ds(at, 2 * rows), :]
        block = jnp.concatenate([block[:, :rows], block[:, rows:]], -1).reshape(flat, 2 * PLANE)
        high, low = split(block)
        value = dot(mix_back[...], high) + dot(mix_back[...], low)
        for k in range(2):
            out = value[:, k * PLANE : (k + 1) * PLANE].reshape(channels, rows, PLANE)
            local[:, pl.ds(pl.multiple_of(at + k * rows, rows), rows), :] = out
        return carry

    lax.fori_loop(0, half_lines // 2, back, 0, unroll=2)
    join(1, chunks - 1)
    lax.fori_loop(half_lines // 2, 3 * half_lines // 2, back, 0, unroll=2)

    gather_total(1, 1.0 / VOLUME)
    for j in range(1, ns):
        side(1, j).start()

    def reduce(c, carry):
        w_r, w_i = w_re[c], w_im[c]
        u_r, u_i = lined[0], lined[1]
        mixed[0, pl.ds(c, 1), :] = jnp.sum(w_r * u_r + w_i * u_i, 0, keepdims=True)
        mixed[1, pl.ds(c, 1), :] = jnp.sum(w_r * u_i - w_i * u_r, 0, keepdims=True)
        return carry

    lax.fori_loop(0, channels, reduce, 0)
    scatter_mixed(1)
    lax.fori_loop(3 * half_lines // 2, 2 * half_lines, back, 0, unroll=2)
    relay(1, 0)

    def term(c, carry):
        real = jnp.zeros((channels, count), F32)
        imag = jnp.zeros((channels, count), F32)
        for s in range(ns):
            a_r, a_i = got[0, s, 0, pl.ds(c, 1), :], got[0, s, 1, pl.ds(c, 1), :]
            b_r, b_i = got[1, s, 0], got[1, s, 1]
            real = real + (a_r * b_r + a_i * b_i)
            imag = imag + (a_r * b_i - a_i * b_r)
        grad[c, :, 0, :] = real
        grad[c, :, 1, :] = imag
        return carry

    def last(k, carry):
        @pl.when(k + 1 < chunks)
        def _():
            relay(1, k + 1)

        @pl.when(k + 1 == chunks)
        def _():
            for e in range(2):
                for j in range(1, ns):
                    side(e, j).wait()
                got[e, 0] = spec[e, mine]
            lax.fori_loop(0, channels, term, 0)

        arrived(1, k)
        inverse_depth(modes[1, k].reshape(n * own_rows, GROUP * XY), depth_i, grid)
        for p in range(GROUP // 2):
            res = inverse_pair(inv, grid, p)
            for h in range(2):
                c = k * GROUP + 2 * p + h
                out[c] = (res[:, h * PLANE : (h + 1) * PLANE] + local[c]).astype(BF16)
        return carry

    lax.fori_loop(0, chunks, last, 0)


def store_kernel(*refs):
    sources, goals, sem = refs[:3], refs[3:6], refs[6]
    copies = [pltpu.make_async_copy(a, b, sem.at[i]) for i, (a, b) in enumerate(zip(sources, goals))]
    for copy in copies:
        copy.start()
    for copy in copies:
        copy.wait()


def shards(fields, cotangent, spectral_weight, point_weight, point_bias):
    _, rows, channels, columns = fields.shape
    n = lax.axis_size("space")
    ns = lax.axis_size("sample")
    forward, inverse, depth_f, depth_i = [jnp.asarray(t) for t in tables(rows, n)]
    cells = NY * rows
    chunks = channels // GROUP
    chips = n // 2
    owned = MT * MZ // n
    own_rows = 2 * owned
    width = GROUP * XY
    flat = channels * rows
    count = owned * XY // ns
    copies = np.repeat(np.eye(channels), rows, 0).astype(BF16)
    same = np.tile(np.eye(rows), (channels, channels)).astype(BF16)

    def by_channel(value):
        value = value[0].reshape(rows, channels, NY, PLANE)
        return jnp.transpose(value, (1, 2, 0, 3)).reshape(channels, cells, PLANE)

    def by_row(value):
        value = jnp.transpose(value.reshape(channels, NY, rows, PLANE), (2, 0, 1, 3))
        return value.reshape(1, rows, channels, columns)

    weight = jnp.transpose(spectral_weight, (1, 2, 0, 3))
    vmem, dma = pltpu.VMEM, pltpu.SemaphoreType.DMA
    any_spec, vmem_spec = pl.BlockSpec(memory_space=pltpu.HBM), pl.BlockSpec(memory_space=vmem)
    kept = (ns, 2, channels, count)
    modes_shape = (chunks, n, own_rows, width)

    smalls = [depth_f, depth_i, point_weight, point_bias[None], copies, copies.T, same]
    act, grad_in, grad = pl.pallas_call(
        functools.partial(main_kernel, n, ns),
        out_shape=[
            vmem((channels, cells, PLANE), BF16),
            vmem((channels, cells, PLANE), BF16),
            vmem((channels, channels, 2, count), F32),
        ],
        in_specs=[any_spec] * 12,
        out_specs=[vmem_spec] * 3,
        scratch_shapes=[vmem(t.shape, t.dtype) for t in smalls] + [
            vmem((channels, cells, PLANE), BF16),
            vmem((channels, cells, PLANE), BF16),
            vmem(weight.shape, BF16),
            vmem(forward.shape[1:], BF16),
            vmem(inverse.shape[1:], BF16),
            vmem((channels, cells, PLANE), F32),
            vmem((channels, cells, PLANE), F32),
            vmem((GROUP, XY, 2 * PLANE), BF16),
            vmem((GROUP, XY, 2 * PLANE), BF16),
            vmem((GROUP, 6 * XY, PLANE), BF16),
            vmem((cells, 2 * PLANE), F32),
            vmem((flat, flat), BF16),
            vmem((flat, flat), BF16),
            vmem((flat, PLANE), F32),
            vmem((channels, 2, owned * XY), F32),
            vmem((channels, channels, owned * XY), F32),
            vmem((channels, channels, owned * XY), F32),
            vmem((chunks, 2, chips * own_rows, width), F32),
            vmem((2, chunks, chips * own_rows, width), F32),
            vmem((2, chunks, chips, own_rows, width), F32),
            vmem((2, chunks, chips - 1, own_rows, width), F32),
            vmem((2,) + modes_shape, F32),
            vmem((GROUP, own_rows, XY), F32),
            vmem((2, channels, owned * XY), F32),
            vmem((2, channels, owned * XY), F32),
            vmem((2,) + kept, F32),
            vmem((2,) + kept, F32),
            dma((2, chunks)), dma((3,)), dma((7,)),
            dma((2, chunks)), dma((2, chunks)),
            dma((2, chunks, chips)), dma((2, chunks, chips)),
            dma((2, chunks, chips)), dma((2, chunks, chips)),
            dma((2, chunks, chips)), dma((2, chunks, chips)),
            dma((2, ns)), dma((2, ns)),
        ],
        compiler_params=pltpu.CompilerParams(
            vmem_limit_bytes=VMEM_LIMIT, collective_id=0, has_side_effects=True
        ),
    )(
        by_channel(fields), by_channel(cotangent), weight, forward, inverse, *smalls
    )

    act, grad_in, grad = pl.pallas_call(
        store_kernel,
        out_shape=[jax.ShapeDtypeStruct(v.shape, v.dtype) for v in (act, grad_in, grad)],
        in_specs=[vmem_spec] * 3,
        out_specs=[any_spec] * 3,
        scratch_shapes=[dma((3,))],
        compiler_params=pltpu.CompilerParams(vmem_limit_bytes=512 * 1024),
    )(act, grad_in, grad)
    return by_row(act), by_row(grad_in), jnp.transpose(grad, (2, 0, 1, 3))


def solution(mesh):
    return jax.shard_map(
        shards,
        mesh=mesh,
        in_specs=(
            P("sample", "space", None, None),
            P("sample", "space", None, None),
            P(None, None, None, "space"),
            P(),
            P(),
        ),
        out_specs=(
            P("sample", "space", None, None),
            P("sample", "space", None, None),
            P(None, None, None, ("space", "sample")),
        ),
        check_vma=False,
    )
```

```python
import functools
import math

import jax
import jax.numpy as jnp
import numpy as np
from jax import lax
from jax.experimental import pallas as pl
from jax.experimental.pallas import tpu as pltpu
from jax.sharding import PartitionSpec as P

NX, NY, NZ, NT = 64, 64, 32, 4
MX, MY, MZ, MT = 12, 12, 8, 4
VOLUME = NX * NY * NZ * NT
PLANE = NZ * NT
XY = MX * MY
BF16, F32 = jnp.bfloat16, jnp.float32
VMEM_LIMIT = 60_970_000
GROUP = 4
MESH = pl.DeviceIdType.MESH


def signed(modes):
    index = np.arange(modes)
    return np.where(index < modes // 2, index, index - modes)


def split_np(table):
    high = table.astype(np.float32).astype(BF16)
    low = (table - high.astype(np.float64)).astype(np.float32).astype(BF16)
    return high, low


def tables(rows, space):
    fy, fx = signed(MY), signed(MX)
    y = np.arange(NY)
    x = np.arange(space * rows).reshape(space, rows)
    phi = 2 * np.pi * (
        (fy.reshape(1, MY, 1, 1, 1) * y.reshape(1, 1, 1, NY, 1) % NY) / NY
        + (fx.reshape(1, 1, MX, 1, 1) * x.reshape(space, 1, 1, 1, rows) % NX) / NX
    ).reshape(space, XY, NY * rows)
    plane = np.concatenate([np.cos(phi), np.sin(phi)], 1)
    hi, lo = split_np(plane)
    forward = np.concatenate([hi, lo], 1)
    turned = lambda t: np.transpose(t, (0, 2, 1))
    inverse = np.concatenate([turned(hi), turned(lo), turned(hi)], 2)
    fz, ft = signed(MZ), signed(MT)
    z, t = np.arange(NZ), np.arange(NT)
    psi = 2 * np.pi * (
        fz.reshape(MZ, 1, 1, 1) * z.reshape(1, 1, NZ, 1) / NZ
        + ft.reshape(1, MT, 1, 1) * t.reshape(1, 1, 1, NT) / NT
    ).reshape(space, MZ * MT // space, PLANE)
    cos, sin = np.cos(psi), np.sin(psi)
    depth = np.stack(
        [np.concatenate([cos, -sin], -1), np.concatenate([-sin, -cos], -1)], 1
    ).reshape(space, 2 * MZ * MT // space, 2 * PLANE)
    dhi, dlo = split_np(depth)
    flat = lambda t: t.reshape(2 * MZ * MT, 2 * PLANE)
    by_core = lambda t: flat(np.concatenate([t[0::2], t[1::2]], 0))
    depth_forward = np.concatenate([by_core(dhi), by_core(dlo)], 0)
    depth_inverse = np.concatenate([flat(dhi), flat(dhi), flat(dlo)], 0)
    return forward, inverse, depth_forward, depth_inverse


def split(value):
    high = value.astype(BF16)
    return high, (value - high.astype(F32)).astype(BF16)


def dot(a, b, contract=(1, 0)):
    dims = (((contract[0],), (contract[1],)), ((), ()))
    return lax.dot_general(a, b, dims, preferred_element_type=F32)


def forward_pair(block, fwd, zhi, zlo, p, exact):
    half = fwd.shape[0] // 2
    if exact:
        res = dot(fwd[...], block)
        res = res[:half] + res[half:]
    else:
        high, low = split(block)
        res = dot(fwd[...], high)
        res = res[:half] + res[half:] + dot(fwd[:half], low)
    for k in range(2):
        part = res[:, k * PLANE : (k + 1) * PLANE]
        high, low = split(jnp.concatenate([part[:XY], part[XY:]], -1))
        zhi[2 * p + k] = high
        zlo[2 * p + k] = low


def forward_depth(depth, zhi, zlo):
    rows = depth.shape[0] // 2
    high = zhi[...].reshape(-1, 2 * PLANE)
    low = zlo[...].reshape(-1, 2 * PLANE)
    first = dot(depth[...], high, (1, 1))
    return first[:rows] + first[rows:] + dot(depth[:rows], low, (1, 1))


def inverse_depth(modes, depth, grid):
    high, low = split(modes)
    stacked = jnp.concatenate([high, low, high], 0)
    lines = dot(stacked, depth[...], (0, 0)).reshape(GROUP, XY, 2 * PLANE)
    high, low = split(lines)
    for at, value in ((0, high), (2 * XY, high), (4 * XY, low)):
        grid[:, at : at + XY] = value[:, :, :PLANE]
        grid[:, at + XY : at + 2 * XY] = value[:, :, PLANE:]


def inverse_pair(inv, grid, p):
    return dot(inv[...], jnp.concatenate([grid[2 * p], grid[2 * p + 1]], -1))


def main_kernel(
    n, ns,
    fields_h, cot_h, weight_h, fwd_h, inv_h, *refs,
):
    smalls_h, (act, out, grad), smalls, refs = refs[:7], refs[7:10], refs[10:17], refs[17:]
    depth_f, depth_i, point, bias_row, copies, copies_t, same = smalls
    (fields, cot, weight, fwd, inv, work, local, zhi, zlo, grid, pre, mix, mix_back, bias, pair_rows, w_re, w_im,
     part, near, joined, recv, modes, stage, lined, mixed, spec, got,
     load_sem, table_sem, small_sem,
     near_send, near_recv, sum_send, sum_recv, all_send, all_recv, relay_send, relay_recv, side_send, side_recv) = refs
    channels, cells, _ = fields.shape
    chunks = channels // GROUP
    rows = cells // NY
    flat = channels * rows
    chips = n // 2
    own_rows = stage.shape[1]
    owned = own_rows // 2
    per = ns // owned
    count = owned * XY // ns
    me = lax.axis_index("space")
    mine = lax.axis_index("sample")
    core = lax.rem(me, 2)
    chip = (me - core) // 2
    sibling = me + 1 - 2 * core

    barrier = pltpu.get_barrier_semaphore()
    for k in range(1, n):
        pl.semaphore_signal(barrier, inc=1, device_id={"space": lax.rem(me + k, n)}, device_id_type=MESH)
    for k in range(1, ns):
        pl.semaphore_signal(barrier, inc=1, device_id={"sample": lax.rem(mine + k, ns)}, device_id_type=MESH)

    def group(k):
        return pl.ds(k * GROUP, GROUP)

    def load(src, dst, which, k):
        return pltpu.make_async_copy(src.at[group(k)], dst.at[group(k)], load_sem.at[which, k])

    fwd_load = pltpu.make_async_copy(fwd_h.at[me], fwd, table_sem.at[0])
    inv_load = pltpu.make_async_copy(inv_h.at[me], inv, table_sem.at[1])
    weight_load = pltpu.make_async_copy(weight_h, weight, table_sem.at[2])
    small_loads = [
        pltpu.make_async_copy(src, dst, small_sem.at[i]) for i, (src, dst) in enumerate(zip(smalls_h, smalls))
    ]
    fwd_load.start()
    load(fields_h, fields, 0, 0).start()
    for copy in small_loads:
        copy.start()
    for k in range(1, chunks):
        load(fields_h, fields, 0, k).start()
    weight_load.start()
    inv_load.start()
    for k in range(chunks):
        load(cot_h, cot, 1, k).start()

    def remote(src, dst, send, got_sem, axis, target):
        return pltpu.make_async_remote_copy(
            src_ref=src, dst_ref=dst, send_sem=send, recv_sem=got_sem,
            device_id={axis: target}, device_id_type=MESH,
        )

    def to_sibling(e, k):
        return remote(part.at[k, 1 - core], near.at[e, k], near_send.at[e, k], near_recv.at[e, k], "space", sibling)

    def partner(j):
        if chips == 4:
            pair = (chip, 3 - chip, lax.rem(chip + 2, 4), chip + 1 - 2 * lax.rem(chip, 2))[j]
            return pair, pair
        return lax.rem(chip + j, chips), lax.rem(chip + chips - j, chips)

    def to_owner(e, k, j):
        goal = partner(j)[0]
        return remote(
            joined.at[e, k, goal], recv.at[e, k, j - 1], sum_send.at[e, k, j], sum_recv.at[e, k, j], "space", 2 * goal + core
        )

    def to_all(e, k, j):
        target = 2 * partner(j)[0] + core if j else sibling
        return remote(modes.at[e, k, me], modes.at[e, k, me], all_send.at[e, k, j], all_recv.at[e, k, j], "space", target)

    def to_relay(e, k, j):
        block = modes.at[e, k, 2 * partner(j)[1] + core]
        return remote(block, block, relay_send.at[e, k, j], relay_recv.at[e, k, j], "space", sibling)

    def join(e, k):
        to_sibling(e, k).wait()
        total = part[k, core] + near[e, k]
        for j in range(chips):
            joined[e, k, j] = total[j * own_rows : (j + 1) * own_rows]
        for j in range(1, chips):
            to_owner(e, k, j).start()

    def put_part(k, value):
        half = value.shape[0] // 2
        part[k, 0] = value[:half]
        part[k, 1] = value[half:]

    def spread(matrix, side):
        half = dot(copies[...], matrix, (1, side)).astype(BF16)
        return dot(half, copies_t[...]).astype(BF16) * same[...]

    fwd_load.wait()

    def transform(k):
        load(fields_h, fields, 0, k).wait()
        for p in range(GROUP // 2):
            c = k * GROUP + 2 * p
            forward_pair(jnp.concatenate([fields[c], fields[c + 1]], -1), fwd, zhi, zlo, p, True)

    def first(k, carry):
        transform(k)
        put_part(k, forward_depth(depth_f, zhi, zlo))
        to_sibling(0, k).start()
        join(0, k - 1)
        return carry

    transform(0)
    for copy in small_loads:
        copy.wait()
    put_part(0, forward_depth(depth_f, zhi, zlo))
    pl.semaphore_wait(barrier, n - 1 + ns - 1)
    to_sibling(0, 0).start()
    lax.fori_loop(1, chunks, first, 0)

    mix[...] = spread(point[...], 1)
    mix_back[...] = spread(point[...], 0)
    column = jnp.sum(copies[...].astype(F32) * bias_row[...], -1, keepdims=True)
    bias[...] = jnp.broadcast_to(column, (flat, PLANE))
    join(0, chunks - 1)

    weight_load.wait()

    def widen(c, carry):
        pair_rows[...] = weight[c].astype(F32)
        w_re[c] = pair_rows[:, 0, :]
        w_im[c] = pair_rows[:, 1, :]
        return carry

    lax.fori_loop(0, channels, widen, 0)

    def pointwise(i, carry):
        at = pl.multiple_of(i * 2 * rows, 2 * rows)
        block = fields[:, pl.ds(at, 2 * rows), :].astype(F32)
        block = jnp.concatenate([block[:, :rows], block[:, rows:]], -1).reshape(flat, 2 * PLANE)
        value = dot(mix[...], block.astype(BF16))
        for k in range(2):
            out = value[:, k * PLANE : (k + 1) * PLANE] + bias[...]
            work[:, pl.ds(pl.multiple_of(at + k * rows, rows), rows), :] = out.reshape(channels, rows, PLANE)
        return carry

    half_lines = NY // 4
    lax.fori_loop(0, half_lines, pointwise, 0, unroll=2)

    def gather_total(e, scale, use=None):
        for k in range(chunks):
            for j in range(1, chips):
                to_owner(e, k, j).wait()
            total = joined[e, k, chip]
            for j in range(1, chips):
                total = total + recv[e, k, j - 1]
            total = total * scale
            for g in range(GROUP):
                stage[g] = total[:, g * XY : (g + 1) * XY]
            for j in range(own_rows):
                r, q = j // owned, j % owned
                block = stage[:, j, :]
                lined[r, k * GROUP : (k + 1) * GROUP, q * XY : (q + 1) * XY] = block
                for p in range(per):
                    spec[e, q * per + p, r, k * GROUP : (k + 1) * GROUP] = block[:, p * count : (p + 1) * count]
            if use is not None:
                use(k)

    def side(e, j):
        goal = lax.rem(mine + j, ns)
        return remote(spec.at[e, goal], got.at[e, j], side_send.at[e, j], side_recv.at[e, j], "sample", goal)

    def scatter_mixed(e):
        for k in range(chunks):
            for j in range(own_rows):
                r, q = j // owned, j % owned
                stage[:, j, :] = mixed[r, k * GROUP : (k + 1) * GROUP, q * XY : (q + 1) * XY]
            modes[e, k, me] = jnp.concatenate([stage[g] for g in range(GROUP)], -1)
            for j in list(range(1, chips)) + [0]:
                to_all(e, k, j).start()

    def add(k):
        real, imag = (mixed[0], mixed[1]) if k else (0.0, 0.0)
        for c in range(k * GROUP, (k + 1) * GROUP):
            w_r, w_i = w_re[c], w_im[c]
            s_r, s_i = lined[0, c : c + 1, :], lined[1, c : c + 1, :]
            real = real + (w_r * s_r - w_i * s_i)
            imag = imag + (w_r * s_i + w_i * s_r)
        scale = 1.0 / VOLUME if k == chunks - 1 else 1.0
        mixed[0] = real * scale
        mixed[1] = imag * scale

    gather_total(0, 1.0, add)
    scatter_mixed(0)
    for j in range(1, ns):
        side(0, j).start()
    inv_load.wait()
    lax.fori_loop(half_lines, 2 * half_lines, pointwise, 0, unroll=2)

    def relay(e, k):
        for j in range(1, chips):
            to_all(e, k, j).wait()
            to_relay(e, k, j).start()

    def arrived(e, k):
        to_all(e, k, 0).wait()
        for j in range(1, chips):
            to_relay(e, k, j).wait()

    relay(0, 0)

    def middle(k, carry):
        @pl.when(k + 1 < chunks)
        def _():
            relay(0, k + 1)

        arrived(0, k)
        inverse_depth(modes[0, k].reshape(n * own_rows, GROUP * XY), depth_i, grid)
        load(cot_h, cot, 1, k).wait()
        for p in range(GROUP // 2):
            pre[p] = inverse_pair(inv, grid, p)
        for p in range(GROUP // 2):
            for h in range(2):
                c = k * GROUP + 2 * p + h
                value = pre[p, :, h * PLANE : (h + 1) * PLANE] + work[c]
                phi = 0.5 * (1.0 + lax.erf(value * (1.0 / math.sqrt(2.0))))
                slope = phi + value * jnp.exp(-0.5 * value * value) * (1.0 / math.sqrt(2.0 * math.pi))
                act[c] = (value * phi).astype(BF16)
                work[c] = cot[c].astype(F32) * slope
            c = k * GROUP + 2 * p
            forward_pair(jnp.concatenate([work[c], work[c + 1]], -1), fwd, zhi, zlo, p, False)

        put_part(k, forward_depth(depth_f, zhi, zlo))
        to_sibling(1, k).start()

        @pl.when(k > 0)
        def _():
            join(1, k - 1)

        return carry

    lax.fori_loop(0, chunks, middle, 0)

    def back(i, carry):
        at = pl.multiple_of(i * 2 * rows, 2 * rows)
        block = work[:, pl.ds(at, 2 * rows), :]
        block = jnp.concatenate([block[:, :rows], block[:, rows:]], -1).reshape(flat, 2 * PLANE)
        high, low = split(block)
        value = dot(mix_back[...], high) + dot(mix_back[...], low)
        for k in range(2):
            out = value[:, k * PLANE : (k + 1) * PLANE].reshape(channels, rows, PLANE)
            local[:, pl.ds(pl.multiple_of(at + k * rows, rows), rows), :] = out
        return carry

    lax.fori_loop(0, half_lines // 2, back, 0, unroll=2)
    join(1, chunks - 1)
    lax.fori_loop(half_lines // 2, 3 * half_lines // 2, back, 0, unroll=2)

    gather_total(1, 1.0 / VOLUME)
    for j in range(1, ns):
        side(1, j).start()

    def reduce(c, carry):
        w_r, w_i = w_re[c], w_im[c]
        u_r, u_i = lined[0], lined[1]
        mixed[0, pl.ds(c, 1), :] = jnp.sum(w_r * u_r + w_i * u_i, 0, keepdims=True)
        mixed[1, pl.ds(c, 1), :] = jnp.sum(w_r * u_i - w_i * u_r, 0, keepdims=True)
        return carry

    lax.fori_loop(0, channels, reduce, 0)
    scatter_mixed(1)
    lax.fori_loop(3 * half_lines // 2, 2 * half_lines, back, 0, unroll=2)
    relay(1, 0)

    def term(c, carry):
        real = jnp.zeros((channels, count), F32)
        imag = jnp.zeros((channels, count), F32)
        for s in range(ns):
            a_r, a_i = got[0, s, 0, pl.ds(c, 1), :], got[0, s, 1, pl.ds(c, 1), :]
            b_r, b_i = got[1, s, 0], got[1, s, 1]
            real = real + (a_r * b_r + a_i * b_i)
            imag = imag + (a_r * b_i - a_i * b_r)
        grad[c, :, 0, :] = real
        grad[c, :, 1, :] = imag
        return carry

    def last(k, carry):
        @pl.when(k + 1 < chunks)
        def _():
            relay(1, k + 1)

        @pl.when(k + 1 == chunks)
        def _():
            for e in range(2):
                for j in range(1, ns):
                    side(e, j).wait()
                got[e, 0] = spec[e, mine]
            lax.fori_loop(0, channels, term, 0)

        arrived(1, k)
        inverse_depth(modes[1, k].reshape(n * own_rows, GROUP * XY), depth_i, grid)
        for p in range(GROUP // 2):
            res = inverse_pair(inv, grid, p)
            for h in range(2):
                c = k * GROUP + 2 * p + h
                out[c] = (res[:, h * PLANE : (h + 1) * PLANE] + local[c]).astype(BF16)
        return carry

    lax.fori_loop(0, chunks, last, 0)


def store_kernel(*refs):
    sources, goals, sem = refs[:3], refs[3:6], refs[6]
    copies = []
    for k in range(sem.shape[1]):
        for i in range(3):
            piece = pl.ds(k * GROUP, GROUP)
            copies.append(pltpu.make_async_copy(sources[i].at[piece], goals[i].at[piece], sem.at[i, k]))
    for copy in copies:
        copy.start()
    for copy in copies:
        copy.wait()


def shards(fields, cotangent, spectral_weight, point_weight, point_bias):
    _, rows, channels, columns = fields.shape
    n = lax.axis_size("space")
    ns = lax.axis_size("sample")
    forward, inverse, depth_f, depth_i = [jnp.asarray(t) for t in tables(rows, n)]
    cells = NY * rows
    chunks = channels // GROUP
    chips = n // 2
    owned = MT * MZ // n
    own_rows = 2 * owned
    width = GROUP * XY
    flat = channels * rows
    count = owned * XY // ns
    copies = np.repeat(np.eye(channels), rows, 0).astype(BF16)
    same = np.tile(np.eye(rows), (channels, channels)).astype(BF16)

    def by_channel(value):
        value = value[0].reshape(rows, channels, NY, PLANE)
        return jnp.transpose(value, (1, 2, 0, 3)).reshape(channels, cells, PLANE)

    def by_row(value):
        value = jnp.transpose(value.reshape(channels, NY, rows, PLANE), (2, 0, 1, 3))
        return value.reshape(1, rows, channels, columns)

    weight = jnp.transpose(spectral_weight, (1, 2, 0, 3))
    vmem, dma = pltpu.VMEM, pltpu.SemaphoreType.DMA
    any_spec, vmem_spec = pl.BlockSpec(memory_space=pltpu.HBM), pl.BlockSpec(memory_space=vmem)
    kept = (ns, 2, channels, count)
    modes_shape = (chunks, n, own_rows, width)

    smalls = [depth_f, depth_i, point_weight, point_bias[None], copies, copies.T, same]
    act, grad_in, grad = pl.pallas_call(
        functools.partial(main_kernel, n, ns),
        out_shape=[
            vmem((channels, cells, PLANE), BF16),
            vmem((channels, cells, PLANE), BF16),
            vmem((channels, channels, 2, count), F32),
        ],
        in_specs=[any_spec] * 12,
        out_specs=[vmem_spec] * 3,
        scratch_shapes=[vmem(t.shape, t.dtype) for t in smalls] + [
            vmem((channels, cells, PLANE), BF16),
            vmem((channels, cells, PLANE), BF16),
            vmem(weight.shape, BF16),
            vmem(forward.shape[1:], BF16),
            vmem(inverse.shape[1:], BF16),
            vmem((channels, cells, PLANE), F32),
            vmem((channels, cells, PLANE), F32),
            vmem((GROUP, XY, 2 * PLANE), BF16),
            vmem((GROUP, XY, 2 * PLANE), BF16),
            vmem((GROUP, 6 * XY, PLANE), BF16),
            vmem((GROUP // 2, cells, 2 * PLANE), F32),
            vmem((flat, flat), BF16),
            vmem((flat, flat), BF16),
            vmem((flat, PLANE), F32),
            vmem((channels, 2, owned * XY), F32),
            vmem((channels, channels, owned * XY), F32),
            vmem((channels, channels, owned * XY), F32),
            vmem((chunks, 2, chips * own_rows, width), F32),
            vmem((2, chunks, chips * own_rows, width), F32),
            vmem((2, chunks, chips, own_rows, width), F32),
            vmem((2, chunks, chips - 1, own_rows, width), F32),
            vmem((2,) + modes_shape, F32),
            vmem((GROUP, own_rows, XY), F32),
            vmem((2, channels, owned * XY), F32),
            vmem((2, channels, owned * XY), F32),
            vmem((2,) + kept, F32),
            vmem((2,) + kept, F32),
            dma((2, chunks)), dma((3,)), dma((7,)),
            dma((2, chunks)), dma((2, chunks)),
            dma((2, chunks, chips)), dma((2, chunks, chips)),
            dma((2, chunks, chips)), dma((2, chunks, chips)),
            dma((2, chunks, chips)), dma((2, chunks, chips)),
            dma((2, ns)), dma((2, ns)),
        ],
        compiler_params=pltpu.CompilerParams(
            vmem_limit_bytes=VMEM_LIMIT, collective_id=0, has_side_effects=True
        ),
    )(
        by_channel(fields), by_channel(cotangent), weight, forward, inverse, *smalls
    )

    act, grad_in, grad = pl.pallas_call(
        store_kernel,
        out_shape=[jax.ShapeDtypeStruct(v.shape, v.dtype) for v in (act, grad_in, grad)],
        in_specs=[vmem_spec] * 3,
        out_specs=[any_spec] * 3,
        scratch_shapes=[dma((3, chunks))],
        compiler_params=pltpu.CompilerParams(vmem_limit_bytes=512 * 1024),
    )(act, grad_in, grad)
    return by_row(act), by_row(grad_in), jnp.transpose(grad, (2, 0, 1, 3))


def solution(mesh):
    return jax.shard_map(
        shards,
        mesh=mesh,
        in_specs=(
            P("sample", "space", None, None),
            P("sample", "space", None, None),
            P(None, None, None, "space"),
            P(),
            P(),
        ),
        out_specs=(
            P("sample", "space", None, None),
            P("sample", "space", None, None),
            P(None, None, None, ("space", "sample")),
        ),
        check_vma=False,
    )
```
